128 devices in a mesh: grp: 8 (over x_lo, z), blk: 16 (over y, x_hi, core).
Axes of the slice: x: 4 (x_hi: 2, x_lo: 2; x = x_hi * 2 + x_lo), y: 4, z: 4, core: 2. Of those that a mesh axis runs over, the one named last changes fastest.
Arguments:
- pair_repr: bfloat16 [512, 512, 128], P(('grp', 'blk')), may hold values from -6 to 6
- pair_mask: int32 [512, 512], P(('grp', 'blk')), may hold values 0 or 1
- chain_index: int32 [512], replicated, may hold values from 0 to 3, never falling along the last dimension, each value on 1 to 256 neighbouring positions
- entity_embed: float32 [2, 128], replicated, may hold values from -3 to 3
- input_gain: float32 [2, 128], replicated, may hold values from 0.5 to 1.5
- input_bias: float32 [2, 128], replicated, may hold values from -2 to 2
- left_weight: bfloat16 [2, 128, 256], replicated, may hold values from -0.5 to 0.5
- right_weight: bfloat16 [2, 128, 256], replicated, may hold values from -0.5 to 0.5
- gate_weight: bfloat16 [2, 128, 128], replicated, may hold values from -0.5 to 0.5
- output_gain: float32 [2, 128], replicated, may hold values from 0.5 to 1.5
- output_bias: float32 [2, 128], replicated, may hold values from -2 to 2
- output_weight: bfloat16 [2, 128, 128], replicated, may hold values from -0.5 to 0.5
Outputs:
- pair_out: bfloat16 [512, 512, 128], P(('grp', 'blk'))
The draws below stay inside these ranges and needn't reach their ends.
Inputs may be any that keep to these rules, and one draw needn't show every extreme that they name: `chain_index`: chain numbers never fall along the residues and every one of the 4 chains has at least one residue.
All inputs are finite; a program needn't handle non-finite values. No bound on the sum of `pair_mask` on one device may be relied on, other than what follows from the above.
Results may differ from the reference program's by a relative error of at most 0.0055.
Values may be sent and summed in bfloat16 or wider, within the bound.
A program may use at most 64 MiB of HBM per device.

```python
import math
import jax
import jax.numpy as jnp
import numpy as np
from jax import lax

CHAN = 128
HIDDEN_SIZE = 128
CHAINS = 4
N_RES = 512


def with_ends(values, stream_key, low, high):
    longest = values.shape.index(max(values.shape))
    spots = []
    for shift in (0, 1):
        where = [jax.random.randint(jax.random.fold_in(stream_key, axis), (), 0, length) for axis, length in enumerate(values.shape)]
        where[longest] = (where[longest] + shift) % values.shape[longest]
        spots.append(tuple(where))
    return values.at[spots[0]].set(low).at[spots[1]].set(high)


def block_scale(own_key, shape, cuts, least, high):
    def one(dim, shards_of):
        draws = jax.random.uniform(jax.random.fold_in(jax.random.fold_in(own_key, 6), dim), (shards_of,), jnp.float32, least / len(cuts), high / len(cuts))
        return jnp.repeat(jnp.exp(draws), shape[dim] // shards_of).reshape((-1,) + (1,) * (len(shape) - dim - 1))

    loudness = one(*cuts[0])
    for cut in cuts[1:]:
        loudness = loudness * one(*cut)
    return loudness


def profile(amount, total, bound, slope):
    weights = [(1 << 20) // math.isqrt(standing ** slope) + 1 for standing in range(2, amount + 1)]
    surplus, given = total - bound - (amount - 1), [1] * (amount - 1)
    while surplus > 0:
        movable = [i for i in range(amount - 1) if given[i] < bound]
        mass, left = sum([weights[i] for i in movable]), surplus
        for i in movable:
            extra = min(bound - given[i], max(1, left * weights[i] // mass), surplus)
            given[i] = given[i] + extra
            surplus = surplus - extra
    return np.array([bound] + given)


def uneven_parts(own_key, number_of, total, most, lean):
    if number_of == 2:
        one = jax.random.randint(own_key, (), max(1, total - most), min(most, total - 1) + 1)
        return jnp.stack([one, total - one])
    sizes = jnp.asarray(profile(number_of, total, most, lean), jnp.int32)
    couples = (number_of - 1) // 2
    source_of, sink = sizes[1:1 + 2 * couples:2], sizes[2:2 + 2 * couples:2]
    margin = jnp.minimum(source_of - 1, most - sink)
    moved = jax.random.randint(jax.random.fold_in(own_key, 1), (couples,), 0, 1 << 20) % (margin + 1)
    sizes = sizes.at[1:1 + 2 * couples:2].set(source_of - moved).at[2:2 + 2 * couples:2].set(sink + moved)
    return sizes[jax.random.permutation(jax.random.fold_in(own_key, 2), number_of)]


def scatter_about(own_key, shape, width, limit, cuts=(), dtype=jnp.bfloat16):
    loudness = block_scale(own_key, shape, cuts, -0.22, 0.18) if cuts else 1.0
    entries = jax.random.normal(own_key, shape, jnp.float32) * width * loudness
    return jnp.minimum(jnp.maximum(entries, -limit), limit).astype(dtype)


def setup_inputs(seed: int = 0) -> dict:
    arg_keys = jax.random.split(jax.random.key(seed), 13)
    pair_repr = scatter_about(arg_keys[0], (N_RES, N_RES, CHAN), 1.0, 6.0, ((0, 128),))
    pair_mask = with_ends((jax.random.randint(arg_keys[1], (N_RES, N_RES), 0, 8) < 7).astype(jnp.int32), jax.random.fold_in(arg_keys[1], 1), 0, 1)
    chain_index = jnp.searchsorted(jnp.cumsum(uneven_parts(arg_keys[2], CHAINS, N_RES, N_RES // 2, 2)), jnp.arange(N_RES), side="right").astype(jnp.int32)
    entity_embed = scatter_about(arg_keys[3], (2, CHAN), 0.5, 3.0, (), jnp.float32)
    input_gain = jnp.clip(1.0 + 0.1 * jax.random.normal(arg_keys[4], (2, CHAN), jnp.float32), 0.5, 1.5)
    input_bias = scatter_about(arg_keys[5], (2, CHAN), 0.3, 2.0, (), jnp.float32)
    left_weight = scatter_about(arg_keys[6], (2, CHAN, 2 * HIDDEN_SIZE), CHAN ** -0.5, 0.5)
    right_weight = scatter_about(arg_keys[7], (2, CHAN, 2 * HIDDEN_SIZE), CHAN ** -0.5, 0.5)
    gate_weight = scatter_about(arg_keys[8], (2, CHAN, CHAN), CHAN ** -0.5, 0.5)
    output_gain = jnp.clip(1.0 + 0.1 * jax.random.normal(arg_keys[9], (2, HIDDEN_SIZE), jnp.float32), 0.5, 1.5)
    output_bias = scatter_about(arg_keys[10], (2, HIDDEN_SIZE), 0.3, 2.0, (), jnp.float32)
    output_weight = scatter_about(arg_keys[11], (2, HIDDEN_SIZE, CHAN), HIDDEN_SIZE ** -0.5, 0.5)
    return {"pair_repr": pair_repr, "pair_mask": pair_mask, "chain_index": chain_index, "entity_embed": entity_embed, "input_gain": input_gain, "input_bias": input_bias, "left_weight": left_weight, "right_weight": right_weight, "gate_weight": gate_weight, "output_gain": output_gain, "output_bias": output_bias, "output_weight": output_weight}


def normalize(values, gain_vector, bias_vector, along):
    average = lax.optimization_barrier(jnp.mean(values, axis=along, keepdims=True))
    centered = values - average
    variance = lax.optimization_barrier(jnp.mean(centered * centered, axis=along, keepdims=True))
    return centered * lax.rsqrt(variance + 1e-05) * gain_vector + bias_vector

def edge_block(flat, weight, mask_column, row_block):
    projected = jnp.dot(flat, weight, preferred_element_type=jnp.float32)
    values = jax.nn.sigmoid(projected[:, :HIDDEN_SIZE]) * projected[:, HIDDEN_SIZE:] * mask_column
    return values.astype(jnp.bfloat16).reshape(row_block, N_RES, HIDDEN_SIZE)

def reference(pair_repr, pair_mask, chain_index, entity_embed, input_gain, input_bias, left_weight, right_weight, gate_weight, output_gain, output_bias, output_weight):
    row_block = math.gcd(N_RES, 64)
    block_total = N_RES // row_block
    chain_blocks = chain_index.reshape(block_total, row_block)
    mask_blocks = pair_mask.reshape(block_total, row_block, N_RES)
    forms = ['hik,hjk->hij', 'hki,hkj->hij']
    group = 8
    base = pair_repr
    for block_index in range(2):

        def state_of(block, chains):
            values = block.astype(jnp.float32)
            if block_index == 0:
                same_chain = chains[:, None] == chain_index[None, :]
                values = values + jnp.where(same_chain[:, :, None], entity_embed[1], entity_embed[0])
            return values.reshape(row_block * N_RES, CHAN)

        def normed_of(values):
            return normalize(values, input_gain[block_index], input_bias[block_index], 1).astype(jnp.bfloat16)

        def edges(items):
            block, chains, mask = items
            normed = normed_of(state_of(block, chains))
            mask_column = mask.astype(jnp.float32).reshape(row_block * N_RES, 1)
            left_part = edge_block(normed, left_weight[block_index], mask_column, row_block)
            right_part = edge_block(normed, right_weight[block_index], mask_column, row_block)
            return (left_part, right_part)
        base_blocks = base.reshape(block_total, row_block, N_RES, CHAN)
        left_blocks, right_blocks = lax.map(edges, (base_blocks, chain_blocks, mask_blocks))
        left_plane = left_blocks.reshape(N_RES, N_RES, HIDDEN_SIZE).transpose(2, 0, 1)
        right_plane = right_blocks.reshape(N_RES, N_RES, HIDDEN_SIZE).transpose(2, 0, 1)
        form = forms[block_index]

        def contract(pieces):
            return jnp.einsum(form, pieces[0].astype(jnp.float32), pieces[1].astype(jnp.float32)).astype(jnp.bfloat16)
        product = lax.map(contract, (left_plane.reshape(HIDDEN_SIZE // group, group, N_RES, N_RES), right_plane.reshape(HIDDEN_SIZE // group, group, N_RES, N_RES)))
        product_blocks = product.reshape(HIDDEN_SIZE, block_total, row_block, N_RES).transpose(1, 0, 2, 3)

        def finish(items):
            block, chains, piece = items
            values = state_of(block, chains)
            normed = normed_of(values)
            gating = jax.nn.sigmoid(jnp.dot(normed, gate_weight[block_index], preferred_element_type=jnp.float32))
            flat_product = piece.reshape(HIDDEN_SIZE, row_block * N_RES).astype(jnp.float32)
            normed_out = normalize(flat_product, output_gain[block_index][:, None], output_bias[block_index][:, None], 0).astype(jnp.bfloat16)
            update = lax.dot_general(normed_out, output_weight[block_index], (((0,), (0,)), ((), ())), preferred_element_type=jnp.float32)
            return (values + gating * update).astype(jnp.bfloat16).reshape(row_block, N_RES, CHAN)
        stored = lax.map(finish, (base_blocks, chain_blocks, product_blocks))
        base = lax.optimization_barrier(stored.reshape(N_RES, N_RES, CHAN))
    return base
```

```python
import jax
import jax.numpy as jnp
from jax import lax
from jax.experimental import pallas as pl
from jax.experimental.pallas import tpu as pltpu
from jax.sharding import PartitionSpec as P

F32, BF16 = jnp.float32, jnp.bfloat16
MESH = pl.DeviceIdType.MESH
LANES = 128
CHUNKS = 2
NN, NT = ((1,), (0,)), ((1,), (1,))


def dot(a, b, dims):
    return lax.dot_general(a, b, (dims, ((), ())), preferred_element_type=F32)


def layer_norm(values, gain, bias):
    average = jnp.mean(values, axis=0, keepdims=True)
    centered = values - average
    variance = jnp.mean(centered * centered, axis=0, keepdims=True)
    return (centered * lax.rsqrt(variance + 1e-05) * gain + bias).astype(BF16)


def body(
    x_ref,
    mask_ref,
    own_chain_ref,
    chain_ref,
    embed_ref,
    in_gain_ref,
    in_bias_ref,
    left_ref,
    right_ref,
    gate_ref,
    out_gain_ref,
    out_bias_ref,
    out_w_ref,
    out_ref,
    cols,
    w_in,
    w_out,
    state,
    gating,
    mask_rows,
    spread,
    left_t,
    edge_send,
    edge_recv,
    prod_send,
    prod_recv,
    edge_ssem,
    edge_rsem,
    prod_ssem,
    prod_rsem,
    own_sem,
):
    rows, columns, chan = x_ref.shape
    blocks = columns // LANES
    wide = rows * LANES
    per = blocks // CHUNKS
    blk_count = lax.axis_size("blk")
    devices = lax.axis_size("grp") * blk_count
    plane = devices * rows
    me = lax.axis_index("grp") * blk_count + lax.axis_index("blk")

    def place(index):
        return (index // blk_count, lax.rem(index, blk_count))

    barrier = pltpu.get_barrier_semaphore()

    def greet(step, carry):
        pl.semaphore_signal(
            barrier, inc=1, device_id=place(lax.rem(me + step, devices)), device_id_type=MESH
        )
        return carry

    lax.fori_loop(1, devices, greet, 0)

    eye = (
        lax.broadcasted_iota(jnp.int32, (LANES, LANES), 0)
        == lax.broadcasted_iota(jnp.int32, (LANES, LANES), 1)
    ).astype(BF16)

    def column(vector):
        return jnp.transpose(jnp.broadcast_to(vector, (LANES, chan)))

    def four(block):
        return jnp.concatenate([block] * rows, axis=1)

    def prepare(u):
        for k, ref in enumerate((in_gain_ref, in_bias_ref, out_gain_ref, out_bias_ref)):
            cols[4 * u + k] = column(ref[u : u + 1, :])
        for k in range(2):
            w_in[u, k * LANES : (k + 1) * LANES, :] = jnp.transpose(
                left_ref[u, :, k * LANES : (k + 1) * LANES]
            )
            w_in[u, (2 + k) * LANES : (3 + k) * LANES, :] = jnp.transpose(
                right_ref[u, :, k * LANES : (k + 1) * LANES]
            )
        w_in[u, 4 * LANES :, :] = jnp.transpose(gate_ref[u])
        w_out[u] = jnp.transpose(out_w_ref[u])

    def load(cb):
        span = slice(cb * LANES, (cb + 1) * LANES)
        other, same = cols[8], cols[9]
        parts, masks = [], []
        for r in range(rows):
            flat = dot(eye, x_ref[r, span, :], NT)
            together = chain_ref[cb : cb + 1, :] == own_chain_ref[me * rows + r]
            parts.append(flat + jnp.where(together, same, other))
            masks.append(mask_ref[r : r + 1, span].astype(F32))
        state[cb] = jnp.concatenate(parts, axis=1)
        mask_rows[cb] = jnp.concatenate(masks, axis=1)

    def edges(u, cb):
        normed = layer_norm(state[cb], four(cols[4 * u]), four(cols[4 * u + 1]))
        for side in range(2):
            low = side * 2 * LANES
            gate = dot(w_in[u, low : low + LANES, :], normed, NN)
            value = dot(w_in[u, low + LANES : low + 2 * LANES, :], normed, NN)
            value = jax.nn.sigmoid(gate) * value * mask_rows[cb]
            for r in range(rows):
                spread[side, pl.ds(r, LANES, stride=rows), :] = value[:, r * LANES : (r + 1) * LANES]
            edge_send.at[u, cb, side].reshape(LANES * rows, LANES)[...] = spread[side].astype(BF16)
        gating[cb] = jax.nn.sigmoid(dot(w_in[u, 4 * LANES :, :], normed, NN))

    def finish(u, cb):
        spread[0] = prod_recv.at[u, cb].reshape(LANES * rows, LANES)[...].astype(F32)
        product = jnp.concatenate(
            [spread[0, pl.ds(r, LANES, stride=rows), :] for r in range(rows)], axis=1
        )
        normed = layer_norm(product, four(cols[4 * u + 2]), four(cols[4 * u + 3]))
        update = dot(w_out[u], normed, NN)
        new = (state[cb] + gating[cb] * update).astype(BF16)
        if u == 0:
            state[cb] = new.astype(F32)
        else:
            for r in range(rows):
                out_ref[r, cb * LANES : (cb + 1) * LANES, :] = dot(
                    eye, new[:, r * LANES : (r + 1) * LANES], NT
                ).astype(BF16)

    def edge_parts(u, ch, source, target):
        span = pl.ds(ch * per, per)
        return edge_send.at[u, span, :, source], edge_recv.at[u, span, :, target]

    def prod_parts(u, ch, source, target):
        span = pl.ds(ch * per, per)
        return prod_send.at[u, span, source], prod_recv.at[u, span, target]

    def send_all(parts, u, ch, ssem, rsem):
        def send(step, carry):
            to = lax.rem(me + step, devices)
            source, target = parts(u, ch, to, me)
            pltpu.make_async_remote_copy(
                src_ref=source,
                dst_ref=target,
                send_sem=ssem.at[u, ch],
                recv_sem=rsem.at[u, ch],
                device_id=place(to),
                device_id_type=MESH,
            ).start()
            return carry

        lax.fori_loop(1, devices, send, 0)
        source, target = parts(u, ch, me, me)
        own = pltpu.make_async_copy(source, target, own_sem)
        own.start()
        own.wait()

    def arrival(parts, u, ch, ssem, rsem):
        source, target = parts(u, ch, pl.ds(0, devices - 1), pl.ds(0, devices - 1))
        return pltpu.make_async_remote_copy(
            src_ref=source,
            dst_ref=target,
            send_sem=ssem.at[u, ch],
            recv_sem=rsem.at[u, ch],
            device_id=place(me),
            device_id_type=MESH,
        )

    def plane_of(u, cb, side):
        return edge_recv.at[u, cb, side].reshape(plane, LANES)

    edge_args = (edge_parts,)
    for k in range(2):
        cols[8 + k] = column(embed_ref[k : k + 1, :])
    prepare(0)
    for ch in range(CHUNKS):
        for cb in range(ch * per, (ch + 1) * per):
            load(cb)
            edges(0, cb)
        if ch == 0:
            pl.semaphore_wait(barrier, devices - 1)
        send_all(edge_parts, 0, ch, edge_ssem, edge_rsem)
    prepare(1)

    for u in range(2):
        if u == 0:
            for ch in range(CHUNKS):
                arrival(edge_parts, u, ch, edge_ssem, edge_rsem).wait_recv()
            left = jnp.concatenate([plane_of(0, cb, 0)[...] for cb in range(blocks)], axis=1)
        else:
            for ch in range(CHUNKS):
                arrival(edge_parts, u, ch, edge_ssem, edge_rsem).wait_recv()
                for cb in range(ch * per, (ch + 1) * per):
                    left_t[cb * LANES : (cb + 1) * LANES, :] = jnp.transpose(plane_of(1, cb, 0)[...])
            left = left_t[...]
        for ch in range(CHUNKS):
            for jb in range(ch * per, (ch + 1) * per):
                if u == 0:
                    right = jnp.concatenate(
                        [
                            plane_of(0, cb, 1)[jb * LANES : (jb + 1) * LANES, :]
                            for cb in range(blocks)
                        ],
                        axis=1,
                    )
                    product = dot(left, right, NT)
                else:
                    product = dot(left, plane_of(1, jb, 1)[...], NN)
                prod_send.at[u, jb].reshape(plane, LANES)[...] = product.astype(BF16)
            send_all(prod_parts, u, ch, prod_ssem, prod_rsem)
        for ch in range(CHUNKS):
            arrival(prod_parts, u, ch, prod_ssem, prod_rsem).wait_recv()
            for cb in range(ch * per, (ch + 1) * per):
                finish(u, cb)
                if u == 0:
                    edges(1, cb)
            if u == 0:
                send_all(edge_parts, 1, ch, edge_ssem, edge_rsem)
    for u in range(2):
        for ch in range(CHUNKS):
            arrival(edge_parts, u, ch, edge_ssem, edge_rsem).wait_send()
            arrival(prod_parts, u, ch, prod_ssem, prod_rsem).wait_send()


def shards(
    pair_repr,
    pair_mask,
    chain_index,
    entity_embed,
    input_gain,
    input_bias,
    left_weight,
    right_weight,
    gate_weight,
    output_gain,
    output_bias,
    output_weight,
):
    rows, columns, chan = pair_repr.shape
    devices = lax.axis_size("grp") * lax.axis_size("blk")
    blocks = columns // LANES
    wide = rows * LANES
    vmem = pl.BlockSpec(memory_space=pltpu.VMEM)
    specs = [vmem, vmem, pl.BlockSpec(memory_space=pltpu.SMEM)] + [vmem] * 10
    return pl.pallas_call(
        body,
        out_shape=jax.ShapeDtypeStruct((rows, columns, chan), BF16),
        in_specs=specs,
        out_specs=vmem,
        scratch_shapes=[
            pltpu.VMEM((10, LANES, LANES), F32),
            pltpu.VMEM((2, 5 * LANES, chan), BF16),
            pltpu.VMEM((2, LANES, LANES), BF16),
            pltpu.VMEM((blocks, chan, wide), F32),
            pltpu.VMEM((blocks, chan, wide), F32),
            pltpu.VMEM((blocks, 1, wide), F32),
            pltpu.VMEM((2, LANES * rows, LANES), F32),
            pltpu.VMEM((columns, devices * rows), BF16),
            pltpu.VMEM((2, blocks, 2, LANES, rows, LANES), BF16),
            pltpu.VMEM((2, blocks, 2, devices, rows, LANES), BF16),
            pltpu.VMEM((2, blocks, devices, rows, LANES), BF16),
            pltpu.VMEM((2, blocks, LANES, rows, LANES), BF16),
            pltpu.SemaphoreType.DMA((2, CHUNKS)),
            pltpu.SemaphoreType.DMA((2, CHUNKS)),
            pltpu.SemaphoreType.DMA((2, CHUNKS)),
            pltpu.SemaphoreType.DMA((2, CHUNKS)),
            pltpu.SemaphoreType.DMA,
        ],
        compiler_params=pltpu.CompilerParams(
            collective_id=0, has_side_effects=True, vmem_limit_bytes=40 * 1024 * 1024
        ),
        name="triangle_updates",
    )(
        pair_repr,
        pair_mask,
        chain_index,
        chain_index.reshape(blocks, LANES),
        entity_embed,
        input_gain,
        input_bias,
        left_weight,
        right_weight,
        gate_weight,
        output_gain,
        output_bias,
        output_weight,
    )


def solution(mesh):
    rows = P(("grp", "blk"), None, None)
    placed = (rows, P(("grp", "blk"), None)) + (P(),) * 10
    return jax.shard_map(shards, mesh=mesh, in_specs=placed, out_specs=rows, check_vma=False)
```

```python
import jax
import jax.numpy as jnp
from jax import lax
from jax.experimental import pallas as pl
from jax.experimental.pallas import tpu as pltpu
from jax.sharding import PartitionSpec as P

F32, BF16 = jnp.float32, jnp.bfloat16
MESH = pl.DeviceIdType.MESH
LANES = 128
CHUNKS = 2
NN, NT = ((1,), (0,)), ((1,), (1,))


def dot(a, b, dims):
    return lax.dot_general(a, b, (dims, ((), ())), preferred_element_type=F32)


def layer_norm(values, gain, bias):
    average = jnp.mean(values, axis=0, keepdims=True)
    centered = values - average
    variance = jnp.mean(centered * centered, axis=0, keepdims=True)
    return (centered * lax.rsqrt(variance + 1e-05) * gain + bias).astype(BF16)


def body(
    x_hbm,
    mask_hbm,
    chain_hbm,
    embed_hbm,
    in_gain_hbm,
    in_bias_hbm,
    left_hbm,
    right_hbm,
    gate_hbm,
    out_gain_hbm,
    out_bias_hbm,
    out_w_hbm,
    out_ref,
    x_ref,
    mask_ref,
    chain_ref,
    embed_ref,
    in_gain_ref,
    in_bias_ref,
    left_ref,
    right_ref,
    gate_ref,
    out_gain_ref,
    out_bias_ref,
    out_w_ref,
    own_chain_ref,
    in_sems,
    cols,
    w_in,
    w_out,
    state,
    gating,
    mask_rows,
    spread,
    left_t,
    edge_send,
    edge_recv,
    prod_send,
    prod_recv,
    edge_ssem,
    edge_rsem,
    prod_ssem,
    prod_rsem,
    own_sem,
):
    rows, columns, chan = x_hbm.shape
    blocks = columns // LANES
    per = blocks // CHUNKS
    blk_count = lax.axis_size("blk")
    devices = lax.axis_size("grp") * blk_count
    plane = devices * rows
    me = lax.axis_index("grp") * blk_count + lax.axis_index("blk")

    def place(index):
        return (index // blk_count, lax.rem(index, blk_count))

    loads = {}

    def fetch(name, source, target):
        loads[name] = pltpu.make_async_copy(source, target, in_sems.at[len(loads)])
        loads[name].start()

    def fetched(*wanted):
        for name in wanted:
            loads[name].wait()

    fetch("embed", embed_hbm, embed_ref)
    fetch("in_gain", in_gain_hbm, in_gain_ref)
    fetch("in_bias", in_bias_hbm, in_bias_ref)
    fetch("left", left_hbm, left_ref)
    fetch("right", right_hbm, right_ref)
    fetch("gate", gate_hbm, gate_ref)
    fetch("x", x_hbm, x_ref)
    fetch("chain", chain_hbm, chain_ref)
    fetch("own_chain", chain_hbm, own_chain_ref)
    fetch("mask", mask_hbm, mask_ref)
    fetch("out_gain", out_gain_hbm, out_gain_ref)
    fetch("out_bias", out_bias_hbm, out_bias_ref)
    fetch("out_w", out_w_hbm, out_w_ref)

    barrier = pltpu.get_barrier_semaphore()

    def greet(step, carry):
        pl.semaphore_signal(
            barrier, inc=1, device_id=place(lax.rem(me + step, devices)), device_id_type=MESH
        )
        return carry

    lax.fori_loop(1, devices, greet, 0)

    eye = (
        lax.broadcasted_iota(jnp.int32, (LANES, LANES), 0)
        == lax.broadcasted_iota(jnp.int32, (LANES, LANES), 1)
    ).astype(BF16)

    def column(vector):
        return jnp.transpose(jnp.broadcast_to(vector, (LANES, chan)))

    def four(block):
        return jnp.concatenate([block] * rows, axis=1)

    def prepare_out(u):
        cols[4 * u + 2] = column(out_gain_ref[u : u + 1, :])
        cols[4 * u + 3] = column(out_bias_ref[u : u + 1, :])
        w_out[u] = jnp.transpose(out_w_ref[u])

    def prepare_in(u):
        cols[4 * u] = column(in_gain_ref[u : u + 1, :])
        cols[4 * u + 1] = column(in_bias_ref[u : u + 1, :])
        for k in range(2):
            w_in[u, k * LANES : (k + 1) * LANES, :] = jnp.transpose(
                left_ref[u, :, k * LANES : (k + 1) * LANES]
            )
            w_in[u, (2 + k) * LANES : (3 + k) * LANES, :] = jnp.transpose(
                right_ref[u, :, k * LANES : (k + 1) * LANES]
            )
        w_in[u, 4 * LANES :, :] = jnp.transpose(gate_ref[u])

    def load(cb):
        span = slice(cb * LANES, (cb + 1) * LANES)
        other, same = cols[8], cols[9]
        parts, masks = [], []
        for r in range(rows):
            flat = dot(eye, x_ref[r, span, :], NT)
            together = chain_ref[pl.ds(cb * LANES, LANES)][None, :] == own_chain_ref[me * rows + r]
            parts.append(flat + jnp.where(together, same, other))
            masks.append(mask_ref[r : r + 1, span].astype(F32))
        state[cb] = jnp.concatenate(parts, axis=1)
        mask_rows[cb] = jnp.concatenate(masks, axis=1)

    def edges(u, cb):
        normed = layer_norm(state[cb], four(cols[4 * u]), four(cols[4 * u + 1]))
        for side in range(2):
            low = side * 2 * LANES
            gate = dot(w_in[u, low : low + LANES, :], normed, NN)
            value = dot(w_in[u, low + LANES : low + 2 * LANES, :], normed, NN)
            value = jax.nn.sigmoid(gate) * value * mask_rows[cb]
            for r in range(rows):
                spread[side, pl.ds(r, LANES, stride=rows), :] = value[:, r * LANES : (r + 1) * LANES]
            edge_send.at[u, cb, side].reshape(LANES * rows, LANES)[...] = spread[side].astype(BF16)
        gating[cb] = jax.nn.sigmoid(dot(w_in[u, 4 * LANES :, :], normed, NN))

    def finish(u, cb):
        spread[0] = prod_recv.at[u, cb].reshape(LANES * rows, LANES)[...].astype(F32)
        product = jnp.concatenate(
            [spread[0, pl.ds(r, LANES, stride=rows), :] for r in range(rows)], axis=1
        )
        normed = layer_norm(product, four(cols[4 * u + 2]), four(cols[4 * u + 3]))
        update = dot(w_out[u], normed, NN)
        new = (state[cb] + gating[cb] * update).astype(BF16)
        if u == 0:
            state[cb] = new.astype(F32)
        else:
            for r in range(rows):
                out_ref[r, cb * LANES : (cb + 1) * LANES, :] = dot(
                    eye, new[:, r * LANES : (r + 1) * LANES], NT
                ).astype(BF16)

    def edge_parts(u, ch, source, target):
        span = pl.ds(ch * per, per)
        return edge_send.at[u, span, :, source], edge_recv.at[u, span, :, target]

    def prod_parts(u, ch, source, target):
        span = pl.ds(ch * per, per)
        return prod_send.at[u, span, source], prod_recv.at[u, span, target]

    def send_all(parts, u, ch, ssem, rsem):
        def send(step, carry):
            to = lax.rem(me + step, devices)
            source, target = parts(u, ch, to, me)
            pltpu.make_async_remote_copy(
                src_ref=source,
                dst_ref=target,
                send_sem=ssem.at[u, ch],
                recv_sem=rsem.at[u, ch],
                device_id=place(to),
                device_id_type=MESH,
            ).start()
            return carry

        lax.fori_loop(1, devices, send, 0)
        source, target = parts(u, ch, me, me)
        own = pltpu.make_async_copy(source, target, own_sem)
        own.start()
        own.wait()

    def arrival(parts, u, ch, ssem, rsem):
        source, target = parts(u, ch, pl.ds(0, devices - 1), pl.ds(0, devices - 1))
        return pltpu.make_async_remote_copy(
            src_ref=source,
            dst_ref=target,
            send_sem=ssem.at[u, ch],
            recv_sem=rsem.at[u, ch],
            device_id=place(me),
            device_id_type=MESH,
        )

    def plane_of(u, cb, side):
        return edge_recv.at[u, cb, side].reshape(plane, LANES)

    fetched("embed", "in_gain", "in_bias", "left", "right", "gate")
    for k in range(2):
        cols[8 + k] = column(embed_ref[k : k + 1, :])
    prepare_in(0)
    fetched("x", "chain", "own_chain", "mask")
    for ch in range(CHUNKS):
        for cb in range(ch * per, (ch + 1) * per):
            load(cb)
            edges(0, cb)
        if ch == 0:
            pl.semaphore_wait(barrier, devices - 1)
        send_all(edge_parts, 0, ch, edge_ssem, edge_rsem)
    fetched("out_gain", "out_bias", "out_w")
    prepare_out(0)
    prepare_in(1)
    prepare_out(1)

    for u in range(2):
        if u == 0:
            for ch in range(CHUNKS):
                arrival(edge_parts, u, ch, edge_ssem, edge_rsem).wait_recv()
            left = jnp.concatenate([plane_of(0, cb, 0)[...] for cb in range(blocks)], axis=1)
        else:
            for ch in range(CHUNKS):
                arrival(edge_parts, u, ch, edge_ssem, edge_rsem).wait_recv()
                for cb in range(ch * per, (ch + 1) * per):
                    left_t[cb * LANES : (cb + 1) * LANES, :] = jnp.transpose(plane_of(1, cb, 0)[...])
            left = left_t[...]
        for ch in range(CHUNKS):
            for jb in range(ch * per, (ch + 1) * per):
                if u == 0:
                    right = jnp.concatenate(
                        [
                            plane_of(0, cb, 1)[jb * LANES : (jb + 1) * LANES, :]
                            for cb in range(blocks)
                        ],
                        axis=1,
                    )
                    product = dot(left, right, NT)
                else:
                    product = dot(left, plane_of(1, jb, 1)[...], NN)
                prod_send.at[u, jb].reshape(plane, LANES)[...] = product.astype(BF16)
            send_all(prod_parts, u, ch, prod_ssem, prod_rsem)
        for ch in range(CHUNKS):
            arrival(prod_parts, u, ch, prod_ssem, prod_rsem).wait_recv()
            for cb in range(ch * per, (ch + 1) * per):
                finish(u, cb)
                if u == 0:
                    edges(1, cb)
            if u == 0:
                send_all(edge_parts, 1, ch, edge_ssem, edge_rsem)
    for u in range(2):
        for ch in range(CHUNKS):
            arrival(edge_parts, u, ch, edge_ssem, edge_rsem).wait_send()
            arrival(prod_parts, u, ch, prod_ssem, prod_rsem).wait_send()


def shards(
    pair_repr,
    pair_mask,
    chain_index,
    entity_embed,
    input_gain,
    input_bias,
    left_weight,
    right_weight,
    gate_weight,
    output_gain,
    output_bias,
    output_weight,
):
    rows, columns, chan = pair_repr.shape
    devices = lax.axis_size("grp") * lax.axis_size("blk")
    blocks = columns // LANES
    wide = rows * LANES
    arguments = (
        pair_repr,
        pair_mask,
        chain_index,
        entity_embed,
        input_gain,
        input_bias,
        left_weight,
        right_weight,
        gate_weight,
        output_gain,
        output_bias,
        output_weight,
    )
    return pl.pallas_call(
        body,
        out_shape=jax.ShapeDtypeStruct((rows, columns, chan), BF16),
        in_specs=[pl.BlockSpec(memory_space=pltpu.HBM)] * len(arguments),
        out_specs=pl.BlockSpec(memory_space=pltpu.VMEM),
        scratch_shapes=[pltpu.VMEM(a.shape, a.dtype) for a in arguments]
        + [
            pltpu.SMEM(chain_index.shape, chain_index.dtype),
            pltpu.SemaphoreType.DMA((len(arguments) + 1,)),
            pltpu.VMEM((10, LANES, LANES), F32),
            pltpu.VMEM((2, 5 * LANES, chan), BF16),
            pltpu.VMEM((2, LANES, LANES), BF16),
            pltpu.VMEM((blocks, chan, wide), F32),
            pltpu.VMEM((blocks, chan, wide), F32),
            pltpu.VMEM((blocks, 1, wide), F32),
            pltpu.VMEM((2, LANES * rows, LANES), F32),
            pltpu.VMEM((columns, devices * rows), BF16),
            pltpu.VMEM((2, blocks, 2, LANES, rows, LANES), BF16),
            pltpu.VMEM((2, blocks, 2, devices, rows, LANES), BF16),
            pltpu.VMEM((2, blocks, devices, rows, LANES), BF16),
            pltpu.VMEM((2, blocks, LANES, rows, LANES), BF16),
            pltpu.SemaphoreType.DMA((2, CHUNKS)),
            pltpu.SemaphoreType.DMA((2, CHUNKS)),
            pltpu.SemaphoreType.DMA((2, CHUNKS)),
            pltpu.SemaphoreType.DMA((2, CHUNKS)),
            pltpu.SemaphoreType.DMA,
        ],
        compiler_params=pltpu.CompilerParams(
            collective_id=0, has_side_effects=True, vmem_limit_bytes=40 * 1024 * 1024
        ),
        name="triangle_updates",
    )(*[pltpu.with_memory_space_constraint(a, pltpu.HBM) for a in arguments])


def solution(mesh):
    rows = P(("grp", "blk"), None, None)
    placed = (rows, P(("grp", "blk"), None)) + (P(),) * 10
    return jax.shard_map(shards, mesh=mesh, in_specs=placed, out_specs=rows, check_vma=False)
```

```python
import jax
import jax.numpy as jnp
from jax import lax
from jax.experimental import pallas as pl
from jax.experimental.pallas import tpu as pltpu
from jax.sharding import PartitionSpec as P

F32, BF16 = jnp.float32, jnp.bfloat16
LOGICAL = pl.DeviceIdType.LOGICAL
LANES = 128
EDGE_PARTS = (((0, 4), (4, 8)), ((0, 2), (2, 4), (4, 6), (6, 7), (7, 8)))
PROD_PARTS = (((0, 1), (1, 2), (2, 3), (3, 4)), ((0, 1), (1, 2), (2, 3), (3, 4)))
MOST = 5
UNROLL = 8
NN, NT = ((1,), (0,)), ((1,), (1,))


def dot(a, b, dims):
    return lax.dot_general(a, b, (dims, ((), ())), preferred_element_type=F32)


def layer_norm(values, gain, bias):
    average = jnp.mean(values, axis=0, keepdims=True)
    centered = values - average
    variance = jnp.mean(centered * centered, axis=0, keepdims=True)
    return (centered * lax.rsqrt(variance + 1e-05) * gain + bias).astype(BF16)


def body(
    x_hbm,
    mask_hbm,
    chain_hbm,
    embed_hbm,
    in_gain_hbm,
    in_bias_hbm,
    left_hbm,
    right_hbm,
    gate_hbm,
    out_gain_hbm,
    out_bias_hbm,
    out_w_hbm,
    out_ref,
    x_ref,
    mask_ref,
    chain_ref,
    embed_ref,
    in_gain_ref,
    in_bias_ref,
    left_ref,
    right_ref,
    gate_ref,
    out_gain_ref,
    out_bias_ref,
    out_w_ref,
    own_chain_ref,
    in_sems,
    cols,
    w_in,
    w_out,
    state,
    gating,
    normed_rows,
    mask_rows,
    spread,
    left_t,
    edge_send,
    edge_recv,
    prod_send,
    prod_recv,
    edge_ssem,
    edge_rsem,
    prod_ssem,
    prod_rsem,
    edge_own,
    prod_own,
):
    rows, columns, chan = x_hbm.shape
    blocks = columns // LANES
    blk_count = lax.axis_size("blk")
    devices = lax.axis_size("grp") * blk_count
    plane = devices * rows
    me = lax.axis_index("grp") * blk_count + lax.axis_index("blk")

    loads = {}

    def fetch(name, source, target):
        loads[name] = pltpu.make_async_copy(source, target, in_sems.at[len(loads)])
        loads[name].start()

    def fetched(*wanted):
        for name in wanted:
            loads[name].wait()

    fetch("embed", embed_hbm, embed_ref)
    fetch("in_gain", in_gain_hbm, in_gain_ref)
    fetch("in_bias", in_bias_hbm, in_bias_ref)
    fetch("left", left_hbm, left_ref)
    fetch("right", right_hbm, right_ref)
    fetch("gate", gate_hbm, gate_ref)
    fetch("x", x_hbm, x_ref)
    fetch("chain", chain_hbm, chain_ref)
    fetch("own_chain", chain_hbm, own_chain_ref)
    fetch("mask", mask_hbm, mask_ref)
    fetch("out_gain", out_gain_hbm, out_gain_ref)
    fetch("out_bias", out_bias_hbm, out_bias_ref)
    fetch("out_w", out_w_hbm, out_w_ref)

    barrier = pltpu.get_barrier_semaphore()

    def greet(step, carry):
        pl.semaphore_signal(
            barrier, inc=1, device_id=lax.rem(me + step, devices), device_id_type=LOGICAL
        )
        return carry

    lax.fori_loop(1, devices, greet, 0, unroll=UNROLL)

    eye = (
        lax.broadcasted_iota(jnp.int32, (LANES, LANES), 0)
        == lax.broadcasted_iota(jnp.int32, (LANES, LANES), 1)
    ).astype(BF16)

    def column(vector):
        return jnp.transpose(jnp.broadcast_to(vector, (LANES, chan)))

    def four(block):
        return jnp.concatenate([block] * rows, axis=1)

    def prepare_out(u):
        cols[4 * u + 2] = column(out_gain_ref[u : u + 1, :])
        cols[4 * u + 3] = column(out_bias_ref[u : u + 1, :])
        w_out[u] = jnp.transpose(out_w_ref[u])

    def prepare_in(u):
        cols[4 * u] = column(in_gain_ref[u : u + 1, :])
        cols[4 * u + 1] = column(in_bias_ref[u : u + 1, :])
        for k in range(2):
            w_in[u, k * LANES : (k + 1) * LANES, :] = jnp.transpose(
                left_ref[u, :, k * LANES : (k + 1) * LANES]
            )
            w_in[u, (2 + k) * LANES : (3 + k) * LANES, :] = jnp.transpose(
                right_ref[u, :, k * LANES : (k + 1) * LANES]
            )
        w_in[u, 4 * LANES :, :] = jnp.transpose(gate_ref[u])

    def load(cb):
        span = slice(cb * LANES, (cb + 1) * LANES)
        other, same = cols[8], cols[9]
        parts, masks = [], []
        for r in range(rows):
            flat = dot(eye, x_ref[r, span, :], NT)
            together = chain_ref[pl.ds(cb * LANES, LANES)][None, :] == own_chain_ref[me * rows + r]
            parts.append(flat + jnp.where(together, same, other))
            masks.append(mask_ref[r : r + 1, span].astype(F32))
        state[cb] = jnp.concatenate(parts, axis=1)
        mask_rows[cb] = jnp.concatenate(masks, axis=1)

    def edges(u, cb):
        normed = layer_norm(state[cb], four(cols[4 * u]), four(cols[4 * u + 1]))
        normed_rows[cb] = normed
        for side in range(2):
            low = side * 2 * LANES
            gate = dot(w_in[u, low : low + LANES, :], normed, NN)
            value = dot(w_in[u, low + LANES : low + 2 * LANES, :], normed, NN)
            value = jax.nn.sigmoid(gate) * value * mask_rows[cb]
            for r in range(rows):
                spread[side, pl.ds(r, LANES, stride=rows), :] = value[:, r * LANES : (r + 1) * LANES]
            edge_send.at[u, 2 * cb + side].reshape(LANES * rows, LANES)[...] = spread[side].astype(BF16)

    def gate(u, cb):
        gating[cb] = jax.nn.sigmoid(dot(w_in[u, 4 * LANES :, :], normed_rows[cb], NN))

    def finish(u, cb):
        spread[0] = prod_recv.at[u, cb].reshape(LANES * rows, LANES)[...].astype(F32)
        product = jnp.concatenate(
            [spread[0, pl.ds(r, LANES, stride=rows), :] for r in range(rows)], axis=1
        )
        normed = layer_norm(product, four(cols[4 * u + 2]), four(cols[4 * u + 3]))
        update = dot(w_out[u], normed, NN)
        new = (state[cb] + gating[cb] * update).astype(BF16)
        if u == 0:
            state[cb] = new.astype(F32)
        else:
            for r in range(rows):
                out_ref[r, cb * LANES : (cb + 1) * LANES, :] = dot(
                    eye, new[:, r * LANES : (r + 1) * LANES], NT
                ).astype(BF16)

    edge_stage = (EDGE_PARTS, edge_send, edge_recv, edge_ssem, edge_rsem, edge_own)
    prod_stage = (PROD_PARTS, prod_send, prod_recv, prod_ssem, prod_rsem, prod_own)

    def ends(stage, u, part, source, target):
        parts, sent, received = stage[:3]
        low, high = parts[u][part]
        span = pl.ds(low, high - low)
        return sent.at[u, span, source], received.at[u, span, target]

    def send_all(stage, u, part):
        ssem, rsem, own_sem = stage[3:]
        source, target = ends(stage, u, part, me, me)
        pltpu.make_async_copy(source, target, own_sem.at[u, part]).start()

        def send(step, carry):
            to = lax.rem(me + step, devices)
            source, target = ends(stage, u, part, to, me)
            pltpu.make_async_remote_copy(
                src_ref=source,
                dst_ref=target,
                send_sem=ssem.at[u, part],
                recv_sem=rsem.at[u, part],
                device_id=to,
                device_id_type=LOGICAL,
            ).start()
            return carry

        lax.fori_loop(1, devices, send, 0, unroll=UNROLL)

    def all_of(stage, u, part):
        ssem, rsem = stage[3:5]
        others = pl.ds(0, devices - 1)
        source, target = ends(stage, u, part, others, others)
        return pltpu.make_async_remote_copy(
            src_ref=source,
            dst_ref=target,
            send_sem=ssem.at[u, part],
            recv_sem=rsem.at[u, part],
            device_id=me,
            device_id_type=LOGICAL,
        )

    def receive(stage, u, part):
        source, target = ends(stage, u, part, me, me)
        pltpu.make_async_copy(source, target, stage[5].at[u, part]).wait()
        all_of(stage, u, part).wait_recv()

    def plane_of(u, cb, side):
        return edge_recv.at[u, 2 * cb + side].reshape(plane, LANES)

    fetched("embed", "in_gain", "in_bias", "left", "right", "gate")
    for k in range(2):
        cols[8 + k] = column(embed_ref[k : k + 1, :])
    prepare_in(0)
    fetched("x", "chain", "own_chain", "mask")
    for part, (low, high) in enumerate(EDGE_PARTS[0]):
        for cb in range(low // 2, high // 2):
            load(cb)
            edges(0, cb)
        if part == 0:
            pl.semaphore_wait(barrier, devices - 1)
        send_all(edge_stage, 0, part)
    for cb in range(blocks):
        gate(0, cb)
    fetched("out_gain", "out_bias", "out_w")
    prepare_out(0)
    prepare_in(1)
    prepare_out(1)

    for part in range(len(EDGE_PARTS[0])):
        receive(edge_stage, 0, part)
    left = jnp.concatenate([plane_of(0, cb, 0)[...] for cb in range(blocks)], axis=1)
    for part, (low, high) in enumerate(PROD_PARTS[0]):
        for jb in range(low, high):
            span = slice(jb * LANES, (jb + 1) * LANES)
            right = jnp.concatenate(
                [plane_of(0, cb, 1)[span, :] for cb in range(blocks)], axis=1
            )
            prod_send.at[0, jb].reshape(plane, LANES)[...] = dot(left, right, NT).astype(BF16)
        send_all(prod_stage, 0, part)

    sent = 0
    for part, (low, high) in enumerate(PROD_PARTS[0]):
        receive(prod_stage, 0, part)
        for cb in range(low, high):
            finish(0, cb)
            edges(1, cb)
        while sent < len(EDGE_PARTS[1]) and EDGE_PARTS[1][sent][1] <= 2 * high:
            send_all(edge_stage, 1, sent)
            sent += 1
        for cb in range(low, high):
            gate(1, cb)

    done = 0
    for part, (low, high) in enumerate(EDGE_PARTS[1]):
        receive(edge_stage, 1, part)
        for item in range(low, high):
            if item % 2 == 0:
                cb = item // 2
                left_t[cb * LANES : (cb + 1) * LANES, :] = jnp.transpose(plane_of(1, cb, 0)[...])
        if high < 2 * blocks - 1:
            continue
        while done < len(PROD_PARTS[1]) and 2 * PROD_PARTS[1][done][1] <= high:
            for jb in range(*PROD_PARTS[1][done]):
                product = dot(left_t[...], plane_of(1, jb, 1)[...], NN)
                prod_send.at[1, jb].reshape(plane, LANES)[...] = product.astype(BF16)
            send_all(prod_stage, 1, done)
            done += 1

    for part, (low, high) in enumerate(PROD_PARTS[1]):
        receive(prod_stage, 1, part)
        for cb in range(low, high):
            finish(1, cb)
    for u in range(2):
        for stage in (edge_stage, prod_stage):
            for part in range(len(stage[0][u])):
                all_of(stage, u, part).wait_send()


def shards(
    pair_repr,
    pair_mask,
    chain_index,
    entity_embed,
    input_gain,
    input_bias,
    left_weight,
    right_weight,
    gate_weight,
    output_gain,
    output_bias,
    output_weight,
):
    rows, columns, chan = pair_repr.shape
    devices = lax.axis_size("grp") * lax.axis_size("blk")
    blocks = columns // LANES
    wide = rows * LANES
    arguments = (
        pair_repr,
        pair_mask,
        chain_index,
        entity_embed,
        input_gain,
        input_bias,
        left_weight,
        right_weight,
        gate_weight,
        output_gain,
        output_bias,
        output_weight,
    )
    return pl.pallas_call(
        body,
        out_shape=jax.ShapeDtypeStruct((rows, columns, chan), BF16),
        in_specs=[pl.BlockSpec(memory_space=pltpu.HBM)] * len(arguments),
        out_specs=pl.BlockSpec(memory_space=pltpu.VMEM),
        scratch_shapes=[pltpu.VMEM(a.shape, a.dtype) for a in arguments]
        + [
            pltpu.SMEM(chain_index.shape, chain_index.dtype),
            pltpu.SemaphoreType.DMA((len(arguments) + 1,)),
            pltpu.VMEM((10, LANES, LANES), F32),
            pltpu.VMEM((2, 5 * LANES, chan), BF16),
            pltpu.VMEM((2, LANES, LANES), BF16),
            pltpu.VMEM((blocks, chan, wide), F32),
            pltpu.VMEM((blocks, chan, wide), F32),
            pltpu.VMEM((blocks, chan, wide), BF16),
            pltpu.VMEM((blocks, 1, wide), F32),
            pltpu.VMEM((2, LANES * rows, LANES), F32),
            pltpu.VMEM((columns, devices * rows), BF16),
            pltpu.VMEM((2, 2 * blocks, LANES, rows, LANES), BF16),
            pltpu.VMEM((2, 2 * blocks, devices, rows, LANES), BF16),
            pltpu.VMEM((2, blocks, devices, rows, LANES), BF16),
            pltpu.VMEM((2, blocks, LANES, rows, LANES), BF16),
            pltpu.SemaphoreType.DMA((2, MOST)),
            pltpu.SemaphoreType.DMA((2, MOST)),
            pltpu.SemaphoreType.DMA((2, MOST)),
            pltpu.SemaphoreType.DMA((2, MOST)),
            pltpu.SemaphoreType.DMA((2, MOST)),
            pltpu.SemaphoreType.DMA((2, MOST)),
        ],
        compiler_params=pltpu.CompilerParams(
            collective_id=0, has_side_effects=True, vmem_limit_bytes=40 * 1024 * 1024
        ),
        name="triangle_updates",
    )(*[pltpu.with_memory_space_constraint(a, pltpu.HBM) for a in arguments])


def solution(mesh):
    rows = P(("grp", "blk"), None, None)
    placed = (rows, P(("grp", "blk"), None)) + (P(),) * 10
    return jax.shard_map(shards, mesh=mesh, in_specs=placed, out_specs=rows, check_vma=False)
```

```python
import jax
import jax.numpy as jnp
from jax import lax
from jax.experimental import pallas as pl
from jax.experimental.pallas import tpu as pltpu
from jax.sharding import PartitionSpec as P

F32, BF16 = jnp.float32, jnp.bfloat16
LOGICAL = pl.DeviceIdType.LOGICAL
LANES = 128
UNROLL = 8
NN, NT = ((1,), (0,)), ((1,), (1,))
LEFT, RIGHT = 0, 1
MOVES = (
    ("right0", 0, 2),
    ("right0", 2, 2),
    ("left0", 0, 4),
    ("left0", 4, 4),
    ("prod0", 0, 4),
    ("prod0", 4, 4),
    ("edge1", 0, 6),
    ("edge1", 6, 6),
    ("edge1", 12, 4),
    ("prod1", 0, 1),
    ("prod1", 1, 1),
    ("prod1", 2, 2),
)
SLOT = (((0, 1, 2, 3), (6, 7, 8, 9)), ((4, 5, 12, 13), (10, 11, 14, 15)))


def dot(a, b, dims):
    return lax.dot_general(a, b, (dims, ((), ())), preferred_element_type=F32)


def layer_norm(values, gain, bias):
    average = jnp.mean(values, axis=0, keepdims=True)
    centered = values - average
    variance = jnp.mean(centered * centered, axis=0, keepdims=True)
    return (centered * lax.rsqrt(variance + 1e-05) * gain + bias).astype(BF16)


def body(
    x_hbm,
    mask_hbm,
    chain_hbm,
    embed_hbm,
    in_gain_hbm,
    in_bias_hbm,
    left_hbm,
    right_hbm,
    gate_hbm,
    out_gain_hbm,
    out_bias_hbm,
    out_w_hbm,
    out_ref,
    x_ref,
    mask_ref,
    chain_ref,
    embed_ref,
    in_gain_ref,
    in_bias_ref,
    left_ref,
    right_ref,
    gate_ref,
    out_gain_ref,
    out_bias_ref,
    out_w_ref,
    own_chain_ref,
    in_sems,
    cols,
    w_in,
    w_out,
    state,
    gating,
    normed_rows,
    spread,
    left_t,
    right0_send,
    right0_recv,
    left0_send,
    left0_recv,
    prod0_send,
    prod0_recv,
    edge1_send,
    edge1_recv,
    prod1_send,
    prod1_recv,
    send_sems,
    recv_sems,
    own_sems,
):
    rows, columns, chan = x_hbm.shape
    blocks = columns // LANES
    pairs = rows // 2
    blk_count = lax.axis_size("blk")
    devices = lax.axis_size("grp") * blk_count
    plane = devices * rows
    half = devices * 2
    me = lax.axis_index("grp") * blk_count + lax.axis_index("blk")
    buffers = {
        "right0": (right0_send, right0_recv),
        "left0": (left0_send, left0_recv),
        "prod0": (prod0_send, prod0_recv),
        "edge1": (edge1_send, edge1_recv),
        "prod1": (prod1_send, prod1_recv),
    }

    loads = {}

    def fetch(name, source, target):
        loads[name] = pltpu.make_async_copy(source, target, in_sems.at[len(loads)])
        loads[name].start()

    def fetched(*wanted):
        for name in wanted:
            loads[name].wait()

    fetch("embed", embed_hbm, embed_ref)
    fetch("in_gain", in_gain_hbm, in_gain_ref)
    fetch("in_bias", in_bias_hbm, in_bias_ref)
    fetch("left", left_hbm, left_ref)
    fetch("right", right_hbm, right_ref)
    fetch("gate", gate_hbm, gate_ref)
    fetch("x", x_hbm, x_ref)
    fetch("chain", chain_hbm, chain_ref)
    fetch("own_chain", chain_hbm, own_chain_ref)
    fetch("mask", mask_hbm, mask_ref)
    fetch("out_gain", out_gain_hbm, out_gain_ref)
    fetch("out_bias", out_bias_hbm, out_bias_ref)
    fetch("out_w", out_w_hbm, out_w_ref)

    barrier = pltpu.get_barrier_semaphore()

    def greet(step, carry):
        pl.semaphore_signal(
            barrier, inc=1, device_id=lax.rem(me + step, devices), device_id_type=LOGICAL
        )
        return carry

    lax.fori_loop(1, devices, greet, 0, unroll=UNROLL)

    eye = (
        lax.broadcasted_iota(jnp.int32, (LANES, LANES), 0)
        == lax.broadcasted_iota(jnp.int32, (LANES, LANES), 1)
    ).astype(BF16)

    def column(vector):
        return jnp.transpose(jnp.broadcast_to(vector, (LANES, chan)))

    def four(block):
        return jnp.concatenate([block] * 4, axis=1)

    def lanes(index):
        return slice(index * LANES, (index + 1) * LANES)

    def prepare_out(u):
        cols[4 * u + 2] = column(out_gain_ref[u : u + 1, :])
        cols[4 * u + 3] = column(out_bias_ref[u : u + 1, :])
        w_out[u] = jnp.transpose(out_w_ref[u])

    def prepare_in(u):
        cols[4 * u] = column(in_gain_ref[u : u + 1, :])
        cols[4 * u + 1] = column(in_bias_ref[u : u + 1, :])
        for k in range(2):
            w_in[u, lanes(k), :] = jnp.transpose(left_ref[u, :, lanes(k)])
            w_in[u, lanes(2 + k), :] = jnp.transpose(right_ref[u, :, lanes(k)])
        w_in[u, lanes(4), :] = jnp.transpose(gate_ref[u])

    def load(cb):
        other, same = cols[8], cols[9]
        for r in range(rows):
            flat = dot(eye, x_ref[r, lanes(cb), :], NT)
            together = chain_ref[pl.ds(cb * LANES, LANES)][None, :] == own_chain_ref[me * rows + r]
            state[r, :, lanes(cb)] = flat + jnp.where(together, same, other)

    def edge(u, side, normed, mask):
        low = 2 * side
        gate = dot(w_in[u, lanes(low), :], normed, NN)
        value = dot(w_in[u, lanes(low + 1), :], normed, NN)
        return jax.nn.sigmoid(gate) * value * mask

    def edges_of_columns(cb):
        values = jnp.concatenate([state[r, :, lanes(cb)] for r in range(rows)], axis=1)
        mask = jnp.concatenate([mask_ref[r : r + 1, lanes(cb)] for r in range(rows)], axis=1)
        mask = mask.astype(F32)
        normed = layer_norm(values, four(cols[0]), four(cols[1]))
        for r in range(rows):
            normed_rows[r, :, lanes(cb)] = normed[:, lanes(r)]
        value = edge(0, RIGHT, normed, mask)
        for r in range(rows):
            spread[0, pl.ds(r, LANES, stride=rows), :] = value[:, lanes(r)]
        right0_send.at[cb].reshape(LANES * rows, LANES)[...] = spread[
            0, : LANES * rows, :
        ].astype(BF16)
        value = edge(0, LEFT, normed, mask)
        for pair in range(pairs):
            low = pair * 2 * LANES
            for r in range(2):
                spread[1, pl.ds(low + r, LANES, stride=2), :] = value[:, lanes(2 * pair + r)]
            left0_send.at[pair * blocks + cb].reshape(LANES * 2, LANES)[...] = spread[
                1, low : low + 2 * LANES, :
            ].astype(BF16)

    def edges_of_pair(pair):
        for r in range(2):
            row = 2 * pair + r
            mask = mask_ref[row : row + 1, :].astype(F32)
            normed = layer_norm(state[row], four(cols[4]), four(cols[5]))
            normed_rows[row] = normed
            for side in (LEFT, RIGHT):
                value = edge(1, side, normed, mask)
                for cb in range(blocks):
                    low = cb * 2 * LANES
                    spread[2 + side, pl.ds(low + r, LANES, stride=2), :] = value[:, lanes(cb)]
        for side in (LEFT, RIGHT):
            for cb in range(blocks):
                low = cb * 2 * LANES
                edge1_send.at[SLOT[side][pair][cb]].reshape(LANES * 2, LANES)[...] = spread[
                    2 + side, low : low + 2 * LANES, :
                ].astype(BF16)

    def gates(u, row):
        gating[row] = jax.nn.sigmoid(dot(w_in[u, lanes(4), :], normed_rows[row], NN))

    def updated(u, product, values, gate):
        normed = layer_norm(product, four(cols[4 * u + 2]), four(cols[4 * u + 3]))
        return (values + gate * dot(w_out[u], normed, NN)).astype(BF16)

    def finish_pair(pair):
        for jb in range(blocks):
            low = jb * 2 * LANES
            spread[0, low : low + 2 * LANES, :] = (
                prod0_recv.at[pair * blocks + jb].reshape(LANES * 2, LANES)[...].astype(F32)
            )
        for r in range(2):
            row = 2 * pair + r
            product = jnp.concatenate(
                [
                    spread[0, pl.ds(jb * 2 * LANES + r, LANES, stride=2), :]
                    for jb in range(blocks)
                ],
                axis=1,
            )
            state[row] = updated(0, product, state[row], gating[row]).astype(F32)

    def finish_columns(cb):
        spread[0, : LANES * rows, :] = (
            prod1_recv.at[cb].reshape(LANES * rows, LANES)[...].astype(F32)
        )
        product = jnp.concatenate(
            [spread[0, pl.ds(r, LANES, stride=rows), :] for r in range(rows)], axis=1
        )
        values = jnp.concatenate([state[r, :, lanes(cb)] for r in range(rows)], axis=1)
        gate = jnp.concatenate([gating[r, :, lanes(cb)] for r in range(rows)], axis=1)
        new = updated(1, product, values, gate)
        for r in range(rows):
            out_ref[r, lanes(cb), :] = dot(eye, new[:, lanes(r)], NT).astype(BF16)

    def ends(move, source, target):
        name, low, count = MOVES[move]
        sent, received = buffers[name]
        span = pl.ds(low, count)
        return sent.at[span, source], received.at[span, target]

    def send_all(move):
        source, target = ends(move, me, me)
        pltpu.make_async_copy(source, target, own_sems.at[move]).start()

        def send(step, carry):
            to = lax.rem(me + step, devices)
            source, target = ends(move, to, me)
            pltpu.make_async_remote_copy(
                src_ref=source,
                dst_ref=target,
                send_sem=send_sems.at[move],
                recv_sem=recv_sems.at[move],
                device_id=to,
                device_id_type=LOGICAL,
            ).start()
            return carry

        lax.fori_loop(1, devices, send, 0, unroll=UNROLL)

    def all_of(move):
        others = pl.ds(0, devices - 1)
        source, target = ends(move, others, others)
        return pltpu.make_async_remote_copy(
            src_ref=source,
            dst_ref=target,
            send_sem=send_sems.at[move],
            recv_sem=recv_sems.at[move],
            device_id=me,
            device_id_type=LOGICAL,
        )

    def receive(move):
        source, target = ends(move, me, me)
        pltpu.make_async_copy(source, target, own_sems.at[move]).wait()
        all_of(move).wait_recv()

    fetched("embed", "in_gain", "in_bias", "left", "right", "gate")
    for k in range(2):
        cols[8 + k] = column(embed_ref[k : k + 1, :])
    prepare_in(0)
    fetched("x", "chain", "own_chain", "mask")
    for cb in range(blocks):
        load(cb)
        edges_of_columns(cb)
        if cb == 1:
            pl.semaphore_wait(barrier, devices - 1)
            send_all(0)
    send_all(1)
    send_all(2)
    send_all(3)
    for row in range(rows):
        gates(0, row)
    fetched("out_gain", "out_bias", "out_w")
    prepare_out(0)
    prepare_in(1)
    prepare_out(1)

    receive(0)
    receive(1)
    for pair in range(pairs):
        receive(2 + pair)
        left = jnp.concatenate(
            [left0_recv.at[pair * blocks + cb].reshape(half, LANES)[...] for cb in range(blocks)],
            axis=1,
        )
        for jb in range(blocks):
            right = jnp.concatenate(
                [
                    right0_recv.at[cb].reshape(plane, LANES)[lanes(jb), :]
                    for cb in range(blocks)
                ],
                axis=1,
            )
            prod0_send.at[pair * blocks + jb].reshape(half, LANES)[...] = dot(
                left, right, NT
            ).astype(BF16)
        send_all(4 + pair)

    for pair in range(pairs):
        receive(4 + pair)
        finish_pair(pair)
        edges_of_pair(pair)
        send_all(6 + pair)
        if pair == pairs - 1:
            send_all(8)
        for r in range(2):
            gates(1, 2 * pair + r)

    for pair in range(pairs):
        receive(6 + pair)
        span = slice(pair * half, (pair + 1) * half)
        for cb in range(blocks):
            left_t[lanes(cb), span] = jnp.transpose(
                edge1_recv.at[SLOT[LEFT][pair][cb]].reshape(half, LANES)[...]
            )
    for move in (9, 10, 11):
        if move == 11:
            receive(8)
        for jb in range(MOVES[move][1], MOVES[move][1] + MOVES[move][2]):
            right = jnp.concatenate(
                [
                    edge1_recv.at[SLOT[RIGHT][pair][jb]].reshape(half, LANES)[...]
                    for pair in range(pairs)
                ],
                axis=0,
            )
            prod1_send.at[jb].reshape(plane, LANES)[...] = dot(left_t[...], right, NN).astype(BF16)
        send_all(move)
    for move in (9, 10, 11):
        receive(move)
        for cb in range(MOVES[move][1], MOVES[move][1] + MOVES[move][2]):
            finish_columns(cb)
    for move in range(len(MOVES)):
        all_of(move).wait_send()


def shards(
    pair_repr,
    pair_mask,
    chain_index,
    entity_embed,
    input_gain,
    input_bias,
    left_weight,
    right_weight,
    gate_weight,
    output_gain,
    output_bias,
    output_weight,
):
    rows, columns, chan = pair_repr.shape
    devices = lax.axis_size("grp") * lax.axis_size("blk")
    blocks = columns // LANES
    pairs = rows // 2
    count = len(MOVES)
    arguments = (
        pair_repr,
        pair_mask,
        chain_index,
        entity_embed,
        input_gain,
        input_bias,
        left_weight,
        right_weight,
        gate_weight,
        output_gain,
        output_bias,
        output_weight,
    )
    return pl.pallas_call(
        body,
        out_shape=jax.ShapeDtypeStruct((rows, columns, chan), BF16),
        in_specs=[pl.BlockSpec(memory_space=pltpu.HBM)] * len(arguments),
        out_specs=pl.BlockSpec(memory_space=pltpu.VMEM),
        scratch_shapes=[pltpu.VMEM(a.shape, a.dtype) for a in arguments]
        + [
            pltpu.SMEM(chain_index.shape, chain_index.dtype),
            pltpu.SemaphoreType.DMA((len(arguments) + 1,)),
            pltpu.VMEM((10, LANES, LANES), F32),
            pltpu.VMEM((2, 5 * LANES, chan), BF16),
            pltpu.VMEM((2, LANES, LANES), BF16),
            pltpu.VMEM((rows, chan, columns), F32),
            pltpu.VMEM((rows, chan, columns), F32),
            pltpu.VMEM((rows, chan, columns), BF16),
            pltpu.VMEM((4, 2 * LANES * blocks, LANES), F32),
            pltpu.VMEM((columns, devices * rows), BF16),
            pltpu.VMEM((blocks, LANES, rows, LANES), BF16),
            pltpu.VMEM((blocks, devices, rows, LANES), BF16),
            pltpu.VMEM((pairs * blocks, LANES, 2, LANES), BF16),
            pltpu.VMEM((pairs * blocks, devices, 2, LANES), BF16),
            pltpu.VMEM((pairs * blocks, devices, 2, LANES), BF16),
            pltpu.VMEM((pairs * blocks, LANES, 2, LANES), BF16),
            pltpu.VMEM((2 * pairs * blocks, LANES, 2, LANES), BF16),
            pltpu.VMEM((2 * pairs * blocks, devices, 2, LANES), BF16),
            pltpu.VMEM((blocks, devices, rows, LANES), BF16),
            pltpu.VMEM((blocks, LANES, rows, LANES), BF16),
            pltpu.SemaphoreType.DMA((count,)),
            pltpu.SemaphoreType.DMA((count,)),
            pltpu.SemaphoreType.DMA((count,)),
        ],
        compiler_params=pltpu.CompilerParams(
            collective_id=0, has_side_effects=True, vmem_limit_bytes=40 * 1024 * 1024
        ),
        name="triangle_updates",
    )(*[pltpu.with_memory_space_constraint(a, pltpu.HBM) for a in arguments])


def solution(mesh):
    rows = P(("grp", "blk"), None, None)
    placed = (rows, P(("grp", "blk"), None)) + (P(),) * 10
    return jax.shard_map(shards, mesh=mesh, in_specs=placed, out_specs=rows, check_vma=False)
```

```python
import jax
import jax.numpy as jnp
from jax import lax
from jax.experimental import pallas as pl
from jax.experimental.pallas import tpu as pltpu
from jax.sharding import PartitionSpec as P

F32, BF16 = jnp.float32, jnp.bfloat16
LOGICAL = pl.DeviceIdType.LOGICAL
LANES = 128
UNROLL = 8
NN, NT = ((1,), (0,)), ((1,), (1,))
LEFT, RIGHT = 0, 1
MOVES = (
    ("right0", 0, 2),
    ("right0", 2, 2),
    ("left0", 0, 4),
    ("left0", 4, 4),
    ("prod0", 0, 2),
    ("prod0", 2, 2),
    ("prod0", 4, 4),
    ("edge1", 0, 4),
    ("edge1", 4, 2),
    ("edge1", 6, 6),
    ("edge1", 12, 4),
    ("prod1", 0, 2),
    ("prod1", 2, 2),
)
SLOT = (((0, 1, 4, 5), (6, 7, 8, 9)), ((2, 3, 12, 14), (10, 11, 13, 15)))


def dot(a, b, dims):
    return lax.dot_general(a, b, (dims, ((), ())), preferred_element_type=F32)


def layer_norm(values, gain, bias):
    average = jnp.mean(values, axis=0, keepdims=True)
    centered = values - average
    variance = jnp.mean(centered * centered, axis=0, keepdims=True)
    return (centered * lax.rsqrt(variance + 1e-05) * gain + bias).astype(BF16)


def body(
    x_hbm,
    mask_hbm,
    chain_hbm,
    embed_hbm,
    in_gain_hbm,
    in_bias_hbm,
    left_hbm,
    right_hbm,
    gate_hbm,
    out_gain_hbm,
    out_bias_hbm,
    out_w_hbm,
    out_ref,
    x_ref,
    mask_ref,
    chain_ref,
    embed_ref,
    in_gain_ref,
    in_bias_ref,
    left_ref,
    right_ref,
    gate_ref,
    out_gain_ref,
    out_bias_ref,
    out_w_ref,
    own_chain_ref,
    in_sems,
    cols,
    w_in,
    w_out,
    state,
    gating,
    normed_rows,
    spread,
    left_t,
    right0_send,
    right0_recv,
    left0_send,
    left0_recv,
    prod0_send,
    prod0_recv,
    edge1_send,
    edge1_recv,
    prod1_send,
    prod1_recv,
    send_sems,
    recv_sems,
    own_sems,
):
    rows, columns, chan = x_hbm.shape
    blocks = columns // LANES
    pairs = rows // 2
    blk_count = lax.axis_size("blk")
    devices = lax.axis_size("grp") * blk_count
    plane = devices * rows
    half = devices * 2
    me = lax.axis_index("grp") * blk_count + lax.axis_index("blk")
    buffers = {
        "right0": (right0_send, right0_recv),
        "left0": (left0_send, left0_recv),
        "prod0": (prod0_send, prod0_recv),
        "edge1": (edge1_send, edge1_recv),
        "prod1": (prod1_send, prod1_recv),
    }

    loads = {}

    def fetch(name, source, target):
        loads[name] = pltpu.make_async_copy(source, target, in_sems.at[len(loads)])
        loads[name].start()

    def fetched(*wanted):
        for name in wanted:
            loads[name].wait()

    fetch("embed", embed_hbm, embed_ref)
    fetch("in_gain", in_gain_hbm, in_gain_ref)
    fetch("in_bias", in_bias_hbm, in_bias_ref)
    fetch("left", left_hbm, left_ref)
    fetch("right", right_hbm, right_ref)
    fetch("gate", gate_hbm, gate_ref)
    fetch("x", x_hbm, x_ref)
    fetch("chain", chain_hbm, chain_ref)
    fetch("own_chain", chain_hbm, own_chain_ref)
    fetch("mask", mask_hbm, mask_ref)
    fetch("out_gain", out_gain_hbm, out_gain_ref)
    fetch("out_bias", out_bias_hbm, out_bias_ref)
    fetch("out_w", out_w_hbm, out_w_ref)

    barrier = pltpu.get_barrier_semaphore()

    def greet(step, carry):
        pl.semaphore_signal(
            barrier, inc=1, device_id=lax.rem(me + step, devices), device_id_type=LOGICAL
        )
        return carry

    lax.fori_loop(1, devices, greet, 0, unroll=UNROLL)

    eye = (
        lax.broadcasted_iota(jnp.int32, (LANES, LANES), 0)
        == lax.broadcasted_iota(jnp.int32, (LANES, LANES), 1)
    ).astype(BF16)

    def column(vector):
        return jnp.transpose(jnp.broadcast_to(vector, (LANES, chan)))

    def wide(block, count):
        return jnp.concatenate([block] * count, axis=1)

    def lanes(index):
        return slice(index * LANES, (index + 1) * LANES)

    def prepare_out(u):
        cols[4 * u + 2] = column(out_gain_ref[u : u + 1, :])
        cols[4 * u + 3] = column(out_bias_ref[u : u + 1, :])
        w_out[u] = jnp.transpose(out_w_ref[u])

    def prepare_in(u):
        cols[4 * u] = column(in_gain_ref[u : u + 1, :])
        cols[4 * u + 1] = column(in_bias_ref[u : u + 1, :])
        for k in range(2):
            w_in[u, lanes(k), :] = jnp.transpose(left_ref[u, :, lanes(k)])
            w_in[u, lanes(2 + k), :] = jnp.transpose(right_ref[u, :, lanes(k)])
        w_in[u, lanes(4), :] = jnp.transpose(gate_ref[u])

    def load(cb):
        other, same = cols[8], cols[9]
        for r in range(rows):
            flat = dot(eye, x_ref[r, lanes(cb), :], NT)
            together = chain_ref[pl.ds(cb * LANES, LANES)][None, :] == own_chain_ref[me * rows + r]
            state[r, :, lanes(cb)] = flat + jnp.where(together, same, other)

    def edge(u, side, normed, mask):
        low = 2 * side
        gate = dot(w_in[u, lanes(low), :], normed, NN)
        value = dot(w_in[u, lanes(low + 1), :], normed, NN)
        return jax.nn.sigmoid(gate) * value * mask

    def edges_of_columns(cb):
        values = jnp.concatenate([state[r, :, lanes(cb)] for r in range(rows)], axis=1)
        mask = jnp.concatenate([mask_ref[r : r + 1, lanes(cb)] for r in range(rows)], axis=1)
        mask = mask.astype(F32)
        normed = layer_norm(values, wide(cols[0], rows), wide(cols[1], rows))
        for r in range(rows):
            normed_rows[r, :, lanes(cb)] = normed[:, lanes(r)]
        value = edge(0, RIGHT, normed, mask)
        for r in range(rows):
            spread[0, pl.ds(r, LANES, stride=rows), :] = value[:, lanes(r)]
        right0_send.at[cb].reshape(LANES * rows, LANES)[...] = spread[
            0, : LANES * rows, :
        ].astype(BF16)
        value = edge(0, LEFT, normed, mask)
        for pair in range(pairs):
            low = pair * 2 * LANES
            for r in range(2):
                spread[1, pl.ds(low + r, LANES, stride=2), :] = value[:, lanes(2 * pair + r)]
            left0_send.at[pair * blocks + cb].reshape(LANES * 2, LANES)[...] = spread[
                1, low : low + 2 * LANES, :
            ].astype(BF16)

    def edges_of_pair(pair, spots):
        span = slice(spots[0] * LANES, (spots[-1] + 1) * LANES)
        for r in range(2):
            row = 2 * pair + r
            mask = mask_ref[row : row + 1, span].astype(F32)
            normed = layer_norm(
                state[row, :, span], wide(cols[4], len(spots)), wide(cols[5], len(spots))
            )
            normed_rows[row, :, span] = normed
            for side in (LEFT, RIGHT):
                value = edge(1, side, normed, mask)
                for k, cb in enumerate(spots):
                    low = cb * 2 * LANES
                    spread[2 + side, pl.ds(low + r, LANES, stride=2), :] = value[:, lanes(k)]
        for side in (LEFT, RIGHT):
            for cb in spots:
                low = cb * 2 * LANES
                edge1_send.at[SLOT[side][pair][cb]].reshape(LANES * 2, LANES)[...] = spread[
                    2 + side, low : low + 2 * LANES, :
                ].astype(BF16)

    def gates(u, row):
        gating[row] = jax.nn.sigmoid(dot(w_in[u, lanes(4), :], normed_rows[row], NN))

    def updated(u, product, values, gate):
        count = product.shape[1] // LANES
        gain, bias = wide(cols[4 * u + 2], count), wide(cols[4 * u + 3], count)
        normed = layer_norm(product, gain, bias)
        return (values + gate * dot(w_out[u], normed, NN)).astype(BF16)

    def finish_pair(pair, spots):
        span = slice(spots[0] * LANES, (spots[-1] + 1) * LANES)
        for jb in spots:
            low = jb * 2 * LANES
            spread[0, low : low + 2 * LANES, :] = (
                prod0_recv.at[pair * blocks + jb].reshape(LANES * 2, LANES)[...].astype(F32)
            )
        for r in range(2):
            row = 2 * pair + r
            product = jnp.concatenate(
                [spread[0, pl.ds(jb * 2 * LANES + r, LANES, stride=2), :] for jb in spots],
                axis=1,
            )
            state[row, :, span] = updated(
                0, product, state[row, :, span], gating[row, :, span]
            ).astype(F32)

    def finish_columns(cb):
        spread[0, : LANES * rows, :] = (
            prod1_recv.at[cb].reshape(LANES * rows, LANES)[...].astype(F32)
        )
        product = jnp.concatenate(
            [spread[0, pl.ds(r, LANES, stride=rows), :] for r in range(rows)], axis=1
        )
        values = jnp.concatenate([state[r, :, lanes(cb)] for r in range(rows)], axis=1)
        gate = jnp.concatenate([gating[r, :, lanes(cb)] for r in range(rows)], axis=1)
        new = updated(1, product, values, gate)
        for r in range(rows):
            out_ref[r, lanes(cb), :] = dot(eye, new[:, lanes(r)], NT).astype(BF16)

    def ends(move, source, target):
        name, low, count = MOVES[move]
        sent, received = buffers[name]
        span = pl.ds(low, count)
        return sent.at[span, source], received.at[span, target]

    def send_all(move):
        source, target = ends(move, me, me)
        pltpu.make_async_copy(source, target, own_sems.at[move]).start()

        def send(step, carry):
            to = lax.rem(me + step, devices)
            source, target = ends(move, to, me)
            pltpu.make_async_remote_copy(
                src_ref=source,
                dst_ref=target,
                send_sem=send_sems.at[move],
                recv_sem=recv_sems.at[move],
                device_id=to,
                device_id_type=LOGICAL,
            ).start()
            return carry

        lax.fori_loop(1, devices, send, 0, unroll=UNROLL)

    def all_of(move):
        others = pl.ds(0, devices - 1)
        source, target = ends(move, others, others)
        return pltpu.make_async_remote_copy(
            src_ref=source,
            dst_ref=target,
            send_sem=send_sems.at[move],
            recv_sem=recv_sems.at[move],
            device_id=me,
            device_id_type=LOGICAL,
        )

    def receive(move):
        source, target = ends(move, me, me)
        pltpu.make_async_copy(source, target, own_sems.at[move]).wait()
        all_of(move).wait_recv()

    fetched("embed", "in_gain", "in_bias", "left", "right", "gate")
    for k in range(2):
        cols[8 + k] = column(embed_ref[k : k + 1, :])
    prepare_in(0)
    fetched("x", "chain", "own_chain", "mask")
    for cb in range(blocks):
        load(cb)
        edges_of_columns(cb)
        if cb == 1:
            pl.semaphore_wait(barrier, devices - 1)
            send_all(0)
    send_all(1)
    send_all(2)
    send_all(3)
    for row in range(rows):
        gates(0, row)
    fetched("out_gain", "out_bias", "out_w")
    prepare_out(0)
    prepare_in(1)
    prepare_out(1)

    def products_of_pair(pair, move):
        for slot in spots_of(move):
            jb = slot - pair * blocks
            right = jnp.concatenate(
                [
                    right0_recv.at[cb].reshape(plane, LANES)[lanes(jb), :]
                    for cb in range(blocks)
                ],
                axis=1,
            )
            left = jnp.concatenate(
                [
                    left0_recv.at[pair * blocks + cb].reshape(half, LANES)[...]
                    for cb in range(blocks)
                ],
                axis=1,
            )
            prod0_send.at[slot].reshape(half, LANES)[...] = dot(left, right, NT).astype(BF16)
        send_all(move)

    def spots_of(move):
        name, low, count = MOVES[move]
        return tuple(range(low, low + count))

    receive(0)
    receive(1)
    receive(2)
    products_of_pair(0, 4)
    products_of_pair(0, 5)
    receive(3)
    products_of_pair(1, 6)

    for move, pair, then in ((4, 0, (7,)), (5, 0, (8,)), (6, 1, (9, 10))):
        spots = tuple(slot - pair * blocks for slot in spots_of(move))
        receive(move)
        finish_pair(pair, spots)
        edges_of_pair(pair, spots)
        for following in then:
            send_all(following)
    for row in range(rows):
        gates(1, row)

    for move in (7, 8, 9):
        receive(move)
        for pair in range(pairs):
            for cb in range(blocks):
                if SLOT[LEFT][pair][cb] in spots_of(move):
                    left_t[lanes(cb), pair * half : (pair + 1) * half] = jnp.transpose(
                        edge1_recv.at[SLOT[LEFT][pair][cb]].reshape(half, LANES)[...]
                    )
    arrived = 12
    for move in range(11, len(MOVES)):
        for jb in spots_of(move):
            for last in (10,):
                if SLOT[RIGHT][0][jb] in spots_of(last) and arrived <= SLOT[RIGHT][1][jb]:
                    receive(last)
                    arrived = spots_of(last)[-1] + 1
            right = jnp.concatenate(
                [
                    edge1_recv.at[SLOT[RIGHT][pair][jb]].reshape(half, LANES)[...]
                    for pair in range(pairs)
                ],
                axis=0,
            )
            prod1_send.at[jb].reshape(plane, LANES)[...] = dot(left_t[...], right, NN).astype(BF16)
        send_all(move)
    for move in range(11, len(MOVES)):
        receive(move)
        for cb in spots_of(move):
            finish_columns(cb)
    for move in range(len(MOVES)):
        all_of(move).wait_send()


def shards(
    pair_repr,
    pair_mask,
    chain_index,
    entity_embed,
    input_gain,
    input_bias,
    left_weight,
    right_weight,
    gate_weight,
    output_gain,
    output_bias,
    output_weight,
):
    rows, columns, chan = pair_repr.shape
    devices = lax.axis_size("grp") * lax.axis_size("blk")
    blocks = columns // LANES
    pairs = rows // 2
    count = len(MOVES)
    arguments = (
        pair_repr,
        pair_mask,
        chain_index,
        entity_embed,
        input_gain,
        input_bias,
        left_weight,
        right_weight,
        gate_weight,
        output_gain,
        output_bias,
        output_weight,
    )
    return pl.pallas_call(
        body,
        out_shape=jax.ShapeDtypeStruct((rows, columns, chan), BF16),
        in_specs=[pl.BlockSpec(memory_space=pltpu.HBM)] * len(arguments),
        out_specs=pl.BlockSpec(memory_space=pltpu.VMEM),
        scratch_shapes=[pltpu.VMEM(a.shape, a.dtype) for a in arguments]
        + [
            pltpu.SMEM(chain_index.shape, chain_index.dtype),
            pltpu.SemaphoreType.DMA((len(arguments) + 1,)),
            pltpu.VMEM((10, LANES, LANES), F32),
            pltpu.VMEM((2, 5 * LANES, chan), BF16),
            pltpu.VMEM((2, LANES, LANES), BF16),
            pltpu.VMEM((rows, chan, columns), F32),
            pltpu.VMEM((rows, chan, columns), F32),
            pltpu.VMEM((rows, chan, columns), BF16),
            pltpu.VMEM((4, 2 * LANES * blocks, LANES), F32),
            pltpu.VMEM((columns, devices * rows), BF16),
            pltpu.VMEM((blocks, LANES, rows, LANES), BF16),
            pltpu.VMEM((blocks, devices, rows, LANES), BF16),
            pltpu.VMEM((pairs * blocks, LANES, 2, LANES), BF16),
            pltpu.VMEM((pairs * blocks, devices, 2, LANES), BF16),
            pltpu.VMEM((pairs * blocks, devices, 2, LANES), BF16),
            pltpu.VMEM((pairs * blocks, LANES, 2, LANES), BF16),
            pltpu.VMEM((2 * pairs * blocks, LANES, 2, LANES), BF16),
            pltpu.VMEM((2 * pairs * blocks, devices, 2, LANES), BF16),
            pltpu.VMEM((blocks, devices, rows, LANES), BF16),
            pltpu.VMEM((blocks, LANES, rows, LANES), BF16),
            pltpu.SemaphoreType.DMA((count,)),
            pltpu.SemaphoreType.DMA((count,)),
            pltpu.SemaphoreType.DMA((count,)),
        ],
        compiler_params=pltpu.CompilerParams(
            collective_id=0, has_side_effects=True, vmem_limit_bytes=40 * 1024 * 1024
        ),
        name="triangle_updates",
    )(*[pltpu.with_memory_space_constraint(a, pltpu.HBM) for a in arguments])


def solution(mesh):
    rows = P(("grp", "blk"), None, None)
    placed = (rows, P(("grp", "blk"), None)) + (P(),) * 10
    return jax.shard_map(shards, mesh=mesh, in_specs=placed, out_specs=rows, check_vma=False)
```

```python
import jax
import jax.numpy as jnp
from jax import lax
from jax.experimental import pallas as pl
from jax.experimental.pallas import tpu as pltpu
from jax.sharding import PartitionSpec as P

F32, BF16 = jnp.float32, jnp.bfloat16
LOGICAL = pl.DeviceIdType.LOGICAL
LANES = 128
UNROLL = 8
NN, NT = ((1,), (0,)), ((1,), (1,))
LEFT, RIGHT = 0, 1
MOVES = (
    ("right0", 0, 4),
    ("left0", 0, 4),
    ("left0", 4, 4),
    ("prod0", 0, 2),
    ("prod0", 2, 2),
    ("prod0", 4, 4),
    ("edge1", 0, 4),
    ("edge1", 4, 2),
    ("edge1", 6, 6),
    ("edge1", 12, 4),
    ("prod1", 0, 2),
    ("prod1", 2, 2),
)
SLOT = (((0, 1, 4, 5), (6, 7, 8, 9)), ((2, 3, 12, 14), (10, 11, 13, 15)))


def dot(a, b, dims):
    return lax.dot_general(a, b, (dims, ((), ())), preferred_element_type=F32)


def layer_norm(values, gain, bias):
    average = jnp.mean(values, axis=0, keepdims=True)
    centered = values - average
    variance = jnp.mean(centered * centered, axis=0, keepdims=True)
    return (centered * lax.rsqrt(variance + 1e-05) * gain + bias).astype(BF16)


def body(
    x_hbm,
    mask_hbm,
    chain_hbm,
    embed_hbm,
    in_gain_hbm,
    in_bias_hbm,
    left_hbm,
    right_hbm,
    gate_hbm,
    out_gain_hbm,
    out_bias_hbm,
    out_w_hbm,
    out_ref,
    x_ref,
    mask_ref,
    chain_ref,
    embed_ref,
    in_gain_ref,
    in_bias_ref,
    left_ref,
    right_ref,
    gate_ref,
    out_gain_ref,
    out_bias_ref,
    out_w_ref,
    own_chain_ref,
    in_sems,
    cols,
    w_in,
    w_out,
    state,
    gating,
    normed_rows,
    spread,
    left_t,
    right0_send,
    right0_recv,
    left0_send,
    left0_recv,
    prod0_send,
    prod0_recv,
    edge1_send,
    edge1_recv,
    prod1_send,
    prod1_recv,
    send_sems,
    recv_sems,
    own_sems,
):
    rows, columns, chan = x_hbm.shape
    blocks = columns // LANES
    pairs = rows // 2
    blk_count = lax.axis_size("blk")
    devices = lax.axis_size("grp") * blk_count
    plane = devices * rows
    half = devices * 2
    me = lax.axis_index("grp") * blk_count + lax.axis_index("blk")
    buffers = {
        "right0": (right0_send, right0_recv),
        "left0": (left0_send, left0_recv),
        "prod0": (prod0_send, prod0_recv),
        "edge1": (edge1_send, edge1_recv),
        "prod1": (prod1_send, prod1_recv),
    }

    barrier = pltpu.get_barrier_semaphore()

    def greet(step, carry):
        pl.semaphore_signal(
            barrier, inc=1, device_id=lax.rem(me + step, devices), device_id_type=LOGICAL
        )
        return carry

    lax.fori_loop(1, devices, greet, 0, unroll=UNROLL)

    loads = {}

    def fetch(name, source, target):
        loads[name] = pltpu.make_async_copy(source, target, in_sems.at[len(loads)])
        loads[name].start()

    def fetched(*wanted):
        for name in wanted:
            loads[name].wait()

    fetch("embed", embed_hbm, embed_ref)
    fetch("in_gain", in_gain_hbm, in_gain_ref)
    fetch("in_bias", in_bias_hbm, in_bias_ref)
    fetch("left", left_hbm, left_ref)
    fetch("right", right_hbm, right_ref)
    fetch("gate", gate_hbm, gate_ref)
    fetch("x", x_hbm, x_ref)
    fetch("chain", chain_hbm, chain_ref)
    fetch("own_chain", chain_hbm, own_chain_ref)
    fetch("mask", mask_hbm, mask_ref)
    fetch("out_gain", out_gain_hbm, out_gain_ref)
    fetch("out_bias", out_bias_hbm, out_bias_ref)
    fetch("out_w", out_w_hbm, out_w_ref)

    eye = (
        lax.broadcasted_iota(jnp.int32, (LANES, LANES), 0)
        == lax.broadcasted_iota(jnp.int32, (LANES, LANES), 1)
    ).astype(BF16)

    def column(vector):
        return jnp.transpose(jnp.broadcast_to(vector, (LANES, chan)))

    def wide(block, count):
        return jnp.concatenate([block] * count, axis=1)

    def lanes(index):
        return slice(index * LANES, (index + 1) * LANES)

    def prepare_out(u):
        cols[4 * u + 2] = column(out_gain_ref[u : u + 1, :])
        cols[4 * u + 3] = column(out_bias_ref[u : u + 1, :])
        w_out[u] = jnp.transpose(out_w_ref[u])

    def prepare_in(u):
        cols[4 * u] = column(in_gain_ref[u : u + 1, :])
        cols[4 * u + 1] = column(in_bias_ref[u : u + 1, :])
        for k in range(2):
            w_in[u, lanes(k), :] = jnp.transpose(left_ref[u, :, lanes(k)])
            w_in[u, lanes(2 + k), :] = jnp.transpose(right_ref[u, :, lanes(k)])
        w_in[u, lanes(4), :] = jnp.transpose(gate_ref[u])

    def load(cb):
        other, same = cols[8], cols[9]
        for r in range(rows):
            flat = dot(eye, x_ref[r, lanes(cb), :], NT)
            together = chain_ref[pl.ds(cb * LANES, LANES)][None, :] == own_chain_ref[me * rows + r]
            state[r, :, lanes(cb)] = flat + jnp.where(together, same, other)

    def edge(u, side, normed, mask):
        low = 2 * side
        gate = dot(w_in[u, lanes(low), :], normed, NN)
        value = dot(w_in[u, lanes(low + 1), :], normed, NN)
        return jax.nn.sigmoid(gate) * value * mask

    def edges_of_columns(cb):
        values = jnp.concatenate([state[r, :, lanes(cb)] for r in range(rows)], axis=1)
        mask = jnp.concatenate([mask_ref[r : r + 1, lanes(cb)] for r in range(rows)], axis=1)
        mask = mask.astype(F32)
        normed = layer_norm(values, wide(cols[0], rows), wide(cols[1], rows))
        for r in range(rows):
            normed_rows[r, :, lanes(cb)] = normed[:, lanes(r)]
        value = edge(0, RIGHT, normed, mask)
        for r in range(rows):
            spread[0, pl.ds(r, LANES, stride=rows), :] = value[:, lanes(r)]
        right0_send.at[cb].reshape(LANES * rows, LANES)[...] = spread[
            0, : LANES * rows, :
        ].astype(BF16)
        value = edge(0, LEFT, normed, mask)
        for pair in range(pairs):
            low = pair * 2 * LANES
            for r in range(2):
                spread[1, pl.ds(low + r, LANES, stride=2), :] = value[:, lanes(2 * pair + r)]
            left0_send.at[pair * blocks + cb].reshape(LANES * 2, LANES)[...] = spread[
                1, low : low + 2 * LANES, :
            ].astype(BF16)

    def edges_of_pair(pair, spots):
        span = slice(spots[0] * LANES, (spots[-1] + 1) * LANES)
        count = len(spots)
        own = (2 * pair, 2 * pair + 1)
        values = jnp.concatenate([state[row, :, span] for row in own], axis=1)
        mask = jnp.concatenate([mask_ref[row : row + 1, span] for row in own], axis=1)
        mask = mask.astype(F32)
        normed = layer_norm(values, wide(cols[4], 2 * count), wide(cols[5], 2 * count))
        for r, row in enumerate(own):
            normed_rows[row, :, span] = normed[:, r * count * LANES : (r + 1) * count * LANES]
        for side in (LEFT, RIGHT):
            value = edge(1, side, normed, mask)
            for k, cb in enumerate(spots):
                low = cb * 2 * LANES
                for r in range(2):
                    spread[2 + side, pl.ds(low + r, LANES, stride=2), :] = value[
                        :, lanes(r * count + k)
                    ]
                edge1_send.at[SLOT[side][pair][cb]].reshape(LANES * 2, LANES)[...] = spread[
                    2 + side, low : low + 2 * LANES, :
                ].astype(BF16)

    def gates(u, row):
        gating[row] = jax.nn.sigmoid(dot(w_in[u, lanes(4), :], normed_rows[row], NN))

    def updated(u, product, values, gate):
        count = product.shape[1] // LANES
        gain, bias = wide(cols[4 * u + 2], count), wide(cols[4 * u + 3], count)
        normed = layer_norm(product, gain, bias)
        return (values + gate * dot(w_out[u], normed, NN)).astype(BF16)

    def finish_pair(pair, spots):
        span = slice(spots[0] * LANES, (spots[-1] + 1) * LANES)
        for jb in spots:
            low = jb * 2 * LANES
            spread[0, low : low + 2 * LANES, :] = (
                prod0_recv.at[pair * blocks + jb].reshape(LANES * 2, LANES)[...].astype(F32)
            )
        own = (2 * pair, 2 * pair + 1)
        product = jnp.concatenate(
            [
                spread[0, pl.ds(jb * 2 * LANES + r, LANES, stride=2), :]
                for r in range(2)
                for jb in spots
            ],
            axis=1,
        )
        values = jnp.concatenate([state[row, :, span] for row in own], axis=1)
        gate = jnp.concatenate([gating[row, :, span] for row in own], axis=1)
        new = updated(0, product, values, gate).astype(F32)
        width = len(spots) * LANES
        for r, row in enumerate(own):
            state[row, :, span] = new[:, r * width : (r + 1) * width]

    def finish_columns(cb):
        spread[0, : LANES * rows, :] = (
            prod1_recv.at[cb].reshape(LANES * rows, LANES)[...].astype(F32)
        )
        product = jnp.concatenate(
            [spread[0, pl.ds(r, LANES, stride=rows), :] for r in range(rows)], axis=1
        )
        values = jnp.concatenate([state[r, :, lanes(cb)] for r in range(rows)], axis=1)
        gate = jnp.concatenate([gating[r, :, lanes(cb)] for r in range(rows)], axis=1)
        new = updated(1, product, values, gate)
        for r in range(rows):
            out_ref[r, lanes(cb), :] = dot(eye, new[:, lanes(r)], NT).astype(BF16)

    def ends(move, source, target):
        name, low, count = MOVES[move]
        sent, received = buffers[name]
        span = pl.ds(low, count)
        return sent.at[span, source], received.at[span, target]

    def send_all(move):
        source, target = ends(move, me, me)
        pltpu.make_async_copy(source, target, own_sems.at[move]).start()

        def send(step, carry):
            to = lax.rem(me + step, devices)
            source, target = ends(move, to, me)
            pltpu.make_async_remote_copy(
                src_ref=source,
                dst_ref=target,
                send_sem=send_sems.at[move],
                recv_sem=recv_sems.at[move],
                device_id=to,
                device_id_type=LOGICAL,
            ).start()
            return carry

        lax.fori_loop(1, devices, send, 0, unroll=UNROLL)

    def all_of(move):
        others = pl.ds(0, devices - 1)
        source, target = ends(move, others, others)
        return pltpu.make_async_remote_copy(
            src_ref=source,
            dst_ref=target,
            send_sem=send_sems.at[move],
            recv_sem=recv_sems.at[move],
            device_id=me,
            device_id_type=LOGICAL,
        )

    def receive(move):
        source, target = ends(move, me, me)
        pltpu.make_async_copy(source, target, own_sems.at[move]).wait()
        all_of(move).wait_recv()

    fetched("embed", "in_gain", "in_bias", "left", "right", "gate")
    for k in range(2):
        cols[8 + k] = column(embed_ref[k : k + 1, :])
    prepare_in(0)
    fetched("x", "chain", "own_chain", "mask")
    for cb in range(blocks):
        load(cb)
        edges_of_columns(cb)
    pl.semaphore_wait(barrier, devices - 1)
    send_all(0)
    send_all(1)
    send_all(2)
    for row in range(rows):
        gates(0, row)
    fetched("out_gain", "out_bias", "out_w")
    prepare_out(0)
    prepare_in(1)
    prepare_out(1)

    def products_of_pair(pair, move):
        for slot in spots_of(move):
            jb = slot - pair * blocks
            right = jnp.concatenate(
                [
                    right0_recv.at[cb].reshape(plane, LANES)[lanes(jb), :]
                    for cb in range(blocks)
                ],
                axis=1,
            )
            left = jnp.concatenate(
                [
                    left0_recv.at[pair * blocks + cb].reshape(half, LANES)[...]
                    for cb in range(blocks)
                ],
                axis=1,
            )
            prod0_send.at[slot].reshape(half, LANES)[...] = dot(left, right, NT).astype(BF16)
        send_all(move)

    def spots_of(move):
        name, low, count = MOVES[move]
        return tuple(range(low, low + count))

    receive(0)
    receive(1)
    products_of_pair(0, 3)
    products_of_pair(0, 4)
    receive(2)
    products_of_pair(1, 5)

    for move, pair, then in ((3, 0, (6,)), (4, 0, (7,)), (5, 1, (8, 9))):
        spots = tuple(slot - pair * blocks for slot in spots_of(move))
        receive(move)
        finish_pair(pair, spots)
        edges_of_pair(pair, spots)
        for following in then:
            send_all(following)
    for row in range(rows):
        gates(1, row)

    for move in (6, 7, 8):
        receive(move)
        for pair in range(pairs):
            for cb in range(blocks):
                if SLOT[LEFT][pair][cb] in spots_of(move):
                    left_t[lanes(cb), pair * half : (pair + 1) * half] = jnp.transpose(
                        edge1_recv.at[SLOT[LEFT][pair][cb]].reshape(half, LANES)[...]
                    )
    arrived = 12
    for move in range(10, len(MOVES)):
        for jb in spots_of(move):
            for last in (9,):
                if SLOT[RIGHT][0][jb] in spots_of(last) and arrived <= SLOT[RIGHT][1][jb]:
                    receive(last)
                    arrived = spots_of(last)[-1] + 1
            right = jnp.concatenate(
                [
                    edge1_recv.at[SLOT[RIGHT][pair][jb]].reshape(half, LANES)[...]
                    for pair in range(pairs)
                ],
                axis=0,
            )
            prod1_send.at[jb].reshape(plane, LANES)[...] = dot(left_t[...], right, NN).astype(BF16)
        send_all(move)
    for move in range(10, len(MOVES)):
        receive(move)
        for cb in spots_of(move):
            finish_columns(cb)
    for move in range(len(MOVES)):
        all_of(move).wait_send()


def shards(
    pair_repr,
    pair_mask,
    chain_index,
    entity_embed,
    input_gain,
    input_bias,
    left_weight,
    right_weight,
    gate_weight,
    output_gain,
    output_bias,
    output_weight,
):
    rows, columns, chan = pair_repr.shape
    devices = lax.axis_size("grp") * lax.axis_size("blk")
    blocks = columns // LANES
    pairs = rows // 2
    count = len(MOVES)
    arguments = (
        pair_repr,
        pair_mask,
        chain_index,
        entity_embed,
        input_gain,
        input_bias,
        left_weight,
        right_weight,
        gate_weight,
        output_gain,
        output_bias,
        output_weight,
    )
    return pl.pallas_call(
        body,
        out_shape=jax.ShapeDtypeStruct((rows, columns, chan), BF16),
        in_specs=[pl.BlockSpec(memory_space=pltpu.HBM)] * len(arguments),
        out_specs=pl.BlockSpec(memory_space=pltpu.VMEM),
        scratch_shapes=[pltpu.VMEM(a.shape, a.dtype) for a in arguments]
        + [
            pltpu.SMEM(chain_index.shape, chain_index.dtype),
            pltpu.SemaphoreType.DMA((len(arguments) + 1,)),
            pltpu.VMEM((10, LANES, LANES), F32),
            pltpu.VMEM((2, 5 * LANES, chan), BF16),
            pltpu.VMEM((2, LANES, LANES), BF16),
            pltpu.VMEM((rows, chan, columns), F32),
            pltpu.VMEM((rows, chan, columns), F32),
            pltpu.VMEM((rows, chan, columns), BF16),
            pltpu.VMEM((4, 2 * LANES * blocks, LANES), F32),
            pltpu.VMEM((columns, devices * rows), BF16),
            pltpu.VMEM((blocks, LANES, rows, LANES), BF16),
            pltpu.VMEM((blocks, devices, rows, LANES), BF16),
            pltpu.VMEM((pairs * blocks, LANES, 2, LANES), BF16),
            pltpu.VMEM((pairs * blocks, devices, 2, LANES), BF16),
            pltpu.VMEM((pairs * blocks, devices, 2, LANES), BF16),
            pltpu.VMEM((pairs * blocks, LANES, 2, LANES), BF16),
            pltpu.VMEM((2 * pairs * blocks, LANES, 2, LANES), BF16),
            pltpu.VMEM((2 * pairs * blocks, devices, 2, LANES), BF16),
            pltpu.VMEM((blocks, devices, rows, LANES), BF16),
            pltpu.VMEM((blocks, LANES, rows, LANES), BF16),
            pltpu.SemaphoreType.DMA((count,)),
            pltpu.SemaphoreType.DMA((count,)),
            pltpu.SemaphoreType.DMA((count,)),
        ],
        compiler_params=pltpu.CompilerParams(
            collective_id=0, has_side_effects=True, vmem_limit_bytes=40 * 1024 * 1024
        ),
        name="triangle_updates",
    )(*[pltpu.with_memory_space_constraint(a, pltpu.HBM) for a in arguments])


def solution(mesh):
    rows = P(("grp", "blk"), None, None)
    placed = (rows, P(("grp", "blk"), None)) + (P(),) * 10
    return jax.shard_map(shards, mesh=mesh, in_specs=placed, out_specs=rows, check_vma=False)
```
